32 devices in a mesh: groups: 2 (over y), resp: 4 (over z), section: 4 (over x, core).
Axes of the slice: x: 2, y: 2, z: 4, core: 2. Of those that a mesh axis runs over, the one named last changes fastest.
Arguments:
- completion_rows: bfloat16 [2, 8, 64, 4096], P(None, ('groups', 'resp')), parts along dimension 1, may hold values from -16 to 16
- prompt_pool: bfloat16 [4, 8, 64, 4096], P('section', ('groups', 'resp')), parts along dimension 1, may hold values from -16 to 16
- norm_gain: float32 [4, 4096], P('section'), may hold values from 0.5 to 1.5
- short_taps: float32 [4, 7, 4096], P('section'), may hold values from -2.4 to 2.4
- long_taps: float32 [4, 128, 256], P('section'), may hold values from -0.5 to 0.5
- score_head: float32 [4096], replicated, may hold values from -0.09375 to 0.09375
- live_lengths: int32 [2, 8], P(None, ('groups', 'resp')), parts along dimension 1, may hold values from 16 to 64, as said below
- prompt_owner: int32 [4], P('groups'), parts along dimension 0, may hold values from 0 to 3
- pair_index: int32 [2, 16, 2], P(None, 'groups'), parts along dimension 1, may hold values from 0 to 3
Outputs:
- scores: bfloat16 [2, 8], P(None, ('groups', 'resp')), parts along dimension 1
- gain_grad: float32 [4, 8192], P('section', 'groups'), parts along dimension 1
- short_grad: float32 [4, 14, 4096], P('section', 'groups'), parts along dimension 1
- long_grad: float32 [4, 256, 256], P('section', 'groups'), parts along dimension 1
The draws below stay inside these ranges and needn't reach their ends.
There are 2 independent parts, one for each index of `groups`. The reference program is written for one: setup_inputs(seed, part) draws one part's arguments, and reference() takes and returns one part's arrays. A program takes and returns all parts, laid end to end along the dimension named above; an argument that names none is the same for every part. Nothing has to cross between parts.
Inputs may be any that keep to these rules, and one draw needn't show every extreme that they name: `live_lengths`: live rows of each completion, counted from its first row; in each microbatch one completion has all 64 rows live and another a quarter of 64. `pair_index`: the two members of a pair may coincide.
All inputs are finite; a program needn't handle non-finite values.
Results may differ from the reference program's by a relative error of at most 0.0097.
Values may be sent and summed in bfloat16 or wider, within the bound.
A program may use at most 256 MiB of HBM per device.

```python
import math
import jax
import jax.numpy as jnp
from jax import lax

D = 4096
FG = 256
KL = 128
SHORT = 7
L = 64
PW = 64
MB = 2
COMP = 4
NP = 8
N_RESP = 4
N_SECTION = 4


def rough_rows(key, shape):
    values = jax.random.normal(key, shape, jnp.float32)
    return jnp.clip(values, -16.0, 16.0)


def draw_completion_rows(key, part):
    return rough_rows(jax.random.fold_in(key, 11), (MB, COMP, L, D)).astype(jnp.bfloat16)


def draw_prompt_pool(key, part):
    return rough_rows(jax.random.fold_in(key, 12), (N_SECTION, N_RESP, PW, D)).astype(jnp.bfloat16)


def draw_live_lengths(key, part):
    folded = jax.random.fold_in(key, 21)
    first_key, second_key = jax.random.split(folded)
    base = jax.random.randint(first_key, (MB, COMP), L // 4, L + 1, dtype=jnp.int32)
    orders = jax.vmap(lambda single: jax.random.permutation(single, COMP))(jax.random.split(second_key, MB))
    ranked = jnp.argsort(orders, axis=1, stable=True)
    lengths_out = jnp.where(ranked == 0, L, jnp.where(ranked == 1, L // 4, base))
    return lengths_out.astype(jnp.int32)


def set_ends(array, own_key, low, high):
    spot = [jax.random.randint(jax.random.fold_in(own_key, axis), (), 0, length) for axis, length in enumerate(array.shape)]
    main_axis = array.shape.index(max(array.shape))
    beside = spot[:main_axis] + [(spot[main_axis] + 1) % array.shape[main_axis]] + spot[main_axis + 1:]
    return array.at[tuple(spot)].set(low).at[tuple(beside)].set(high)


def level_of(own_key, dims, pieces, low, largest):
    factor_of = 1.0
    for position, shards_of in pieces:
        draws = jax.random.uniform(jax.random.fold_in(jax.random.fold_in(own_key, 6), position), (shards_of,), jnp.float32, low / len(pieces), largest / len(pieces))
        factor_of = factor_of * jnp.repeat(jnp.exp(draws), dims[position] // shards_of).reshape((-1,) + (1,) * (len(dims) - 1 - position))
    return factor_of


def scatter_about(own_key, shape, width, limit, shards=(), kind=jnp.bfloat16):
    drawn = width * jax.random.normal(own_key, shape, jnp.float32)
    if shards:
        drawn = drawn * level_of(own_key, shape, shards, -0.22, 0.18)
    return jnp.clip(drawn, -limit, limit).astype(kind)


def setup_inputs(seed: int = 0, part: int = 0) -> dict:
    key_of = jax.random.split(jax.random.key(seed), 10)
    part_keys = jax.random.split(jax.random.fold_in(key_of[9], part), 10)
    return {
        "completion_rows": draw_completion_rows(jax.random.fold_in(jax.random.fold_in(key_of[9], part), 71), part),
        "prompt_pool": draw_prompt_pool(jax.random.fold_in(jax.random.fold_in(key_of[9], part), 71), part),
        "norm_gain": jnp.clip(1.0 + 0.1 * jax.random.normal(key_of[2], (N_SECTION, D), jnp.float32), 0.5, 1.5),
        "short_taps": scatter_about(key_of[3], (N_SECTION, SHORT, D), 0.4, 2.4, ((0, 4),), jnp.float32),
        "long_taps": scatter_about(key_of[4], (N_SECTION, KL, FG), KL ** -0.5, 0.5, ((0, 4),), jnp.float32),
        "score_head": scatter_about(key_of[5], (D,), D ** -0.5, 0.09375, (), jnp.float32),
        "live_lengths": draw_live_lengths(jax.random.fold_in(jax.random.fold_in(key_of[9], part), 71), part),
        "prompt_owner": jax.random.randint(part_keys[7], (MB,), 0, N_RESP).astype(jnp.int32),
        "pair_index": set_ends(jax.random.randint(part_keys[8], (MB, NP, 2), 0, COMP), jax.random.fold_in(part_keys[8], 1), 0, COMP - 1).astype(jnp.int32),
    }


def long_conv(values, taps_grouped):
    channels = values.shape[1]
    spread = jnp.repeat(taps_grouped, channels // taps_grouped.shape[1], axis=1)
    count_rows = values.shape[0]
    fft_len = 2 ** int(math.ceil(math.log2(count_rows + spread.shape[0])))
    spectrum = jnp.fft.rfft(values, n=fft_len, axis=0) * jnp.fft.rfft(spread, n=fft_len, axis=0)
    return jnp.fft.irfft(spectrum, n=fft_len, axis=0)[:count_rows]

def mixer(comp_rows, prompt_rows, gain_row, short_row, long_row):
    joined = jnp.concatenate([prompt_rows, comp_rows], axis=0).astype(jnp.float32)
    factor = lax.rsqrt(lax.optimization_barrier(jnp.mean(joined * joined, axis=1, keepdims=True)) + 1e-06)
    normed = joined * factor * gain_row[None, :]
    count_rows = joined.shape[0]
    tap_count = short_row.shape[0]
    padded = jnp.pad(normed, ((tap_count - 1, 0), (0, 0)))
    shorter = jnp.zeros_like(normed)
    for offset in range(tap_count):
        begin = tap_count - 1 - offset
        shorter = shorter + short_row[offset][None, :] * padded[begin:begin + count_rows]
    longer = long_conv(shorter, long_row)
    offset_rows = prompt_rows.shape[0]
    return joined[offset_rows:] + normed[offset_rows:] * longer[offset_rows:]

def pair_slopes(table, pair_index):
    labels = jnp.arange(table.shape[1], dtype=jnp.int32)
    winner = (pair_index[:, :, 0:1] == labels).astype(jnp.float32)
    loser = (pair_index[:, :, 1:2] == labels).astype(jnp.float32)
    margin = lax.optimization_barrier(jnp.sum((winner - loser) * table[:, None, :], axis=2))
    weight = jax.nn.sigmoid(-margin)
    return lax.optimization_barrier(jnp.sum((loser - winner) * weight[:, :, None], axis=1))

def cotangent_rows(slope_arg, head_arg, length_arg, count_rows):
    live = (jnp.arange(count_rows, dtype=jnp.int32) < length_arg).astype(jnp.float32)
    return slope_arg * live[:, None] * head_arg[None, :] / jnp.sqrt(length_arg.astype(jnp.float32))

def reference(completion_rows, prompt_pool, norm_gain, short_taps, long_taps, score_head, live_lengths, prompt_owner, pair_index):
    saved = []
    score_list = []
    for batch_id in range(MB):
        moving = completion_rows[batch_id]
        kept = []
        for section_id in range(N_SECTION):
            prompt_now = lax.dynamic_index_in_dim(prompt_pool[section_id], prompt_owner[batch_id], 0, keepdims=False)
            kept.append((moving, prompt_now))

            def forward_one(rows_arg, prompt_arg=prompt_now, section_arg=section_id):
                return mixer(rows_arg, prompt_arg, norm_gain[section_arg], short_taps[section_arg], long_taps[section_arg]).astype(jnp.bfloat16)
            moving = lax.map(forward_one, moving)
        per_row = jnp.einsum('cld,d->cl', moving.astype(jnp.float32), score_head, precision=lax.Precision.HIGHEST)
        live = jnp.arange(L, dtype=jnp.int32)[None, :] < live_lengths[batch_id][:, None]
        totals = lax.optimization_barrier(jnp.sum(jnp.where(live, per_row, 0.0), axis=1))
        score_list.append(totals / jnp.sqrt(live_lengths[batch_id].astype(jnp.float32)))
        saved.append(kept)
    raw_score = jnp.stack(score_list, axis=0)
    slopes = pair_slopes(raw_score, pair_index)
    gain_acc = [jnp.zeros((D,), jnp.float32) for section_id in range(N_SECTION)]
    short_acc = [jnp.zeros((SHORT, D), jnp.float32) for section_id in range(N_SECTION)]
    long_acc = [jnp.zeros((KL, FG), jnp.float32) for section_id in range(N_SECTION)]
    for batch_id in range(MB):
        cotangent = jax.vmap(cotangent_rows, in_axes=(0, None, 0, None))(slopes[batch_id], score_head, live_lengths[batch_id], L)
        for section_id in reversed(range(N_SECTION)):
            rows_in, prompt_now = saved[batch_id][section_id]

            def visit(carry, item, prompt_arg=prompt_now, section_arg=section_id):
                rows_arg, cot_arg = item

                def local_layer(rows_var, gain_var, short_var, long_var):
                    return mixer(rows_var, prompt_arg, gain_var, short_var, long_var)
                primal, puller = jax.vjp(local_layer, rows_arg, norm_gain[section_arg], short_taps[section_arg], long_taps[section_arg])
                grad_rows, grad_gain, grad_short, grad_long = puller(cot_arg)
                return ((carry[0] + grad_gain, carry[1] + grad_short, carry[2] + grad_long), grad_rows)
            start = (jnp.zeros((D,), jnp.float32), jnp.zeros((SHORT, D), jnp.float32), jnp.zeros((KL, FG), jnp.float32))
            summed, grad_inputs = lax.scan(visit, start, (rows_in, cotangent))
            gain_acc[section_id] = gain_acc[section_id] + summed[0]
            short_acc[section_id] = short_acc[section_id] + summed[1]
            long_acc[section_id] = long_acc[section_id] + summed[2]
            cotangent = lax.optimization_barrier(grad_inputs).astype(jnp.float32)
    return (raw_score.astype(jnp.bfloat16), jnp.stack(gain_acc, axis=0), jnp.stack(short_acc, axis=0), jnp.stack(long_acc, axis=0))
```

```python
import functools

import jax
import jax.numpy as jnp
from jax import lax
from jax.experimental import pallas as pl
from jax.experimental.pallas import tpu as pltpu
from jax.sharding import PartitionSpec as P

LANES = 128
MESH = pl.DeviceIdType.MESH
F32 = jnp.float32
BF16 = jnp.bfloat16


def rows_to_line(block):
    line = jnp.sum(jnp.transpose(block), axis=0, keepdims=True)
    return jnp.broadcast_to(line, (8, LANES))


def line_to_rows(tile):
    return jnp.transpose(jnp.broadcast_to(tile[0:1], (LANES, LANES)))


def kernel(
    dims,
    direct,
    comp_ref,
    prompt_ref,
    gs_hbm,
    taps_hbm,
    chosen_ref,
    head_ref,
    pairs_ref,
    own_pairs_ref,
    live_ref,
    score_ref,
    tiles_ref,
    toep,
    toep_t,
    pool,
    chosen_rows,
    gs_ref,
    taps_ref,
    rows_in,
    short_out,
    long_out,
    fac_p,
    fac_c,
    upstream,
    partial,
    stat_acc,
    score_acc,
    prompt_acc,
    stat_out,
    stat_in,
    resp_out,
    resp_in,
    tiles_own,
    tiles_in,
    tiles_sum,
    local_sem,
    weight_sems,
    pool_send,
    pool_recv,
    stat_sems,
    resp_sems,
    part_sems,
    tile_send,
    tile_recv,
):
    sections, n_resp, micro, length, prompt_len, chans, per_group, width = dims
    groups = LANES // per_group
    blocks = chans // LANES
    group_rows = blocks * groups
    total = prompt_len + length
    me = lax.axis_index("section")
    me_resp = lax.axis_index("resp")
    own_lanes = pl.ds(pl.multiple_of(me * chans, chans), chans)

    def lane_slice(block):
        return pl.ds(pl.multiple_of(block * LANES, LANES), LANES)

    def head_slice(block):
        return pl.ds(pl.multiple_of(me * chans + block * LANES, LANES), LANES)

    def wide_slice(block):
        return pl.ds(pl.multiple_of(block * micro * LANES, LANES), micro * LANES)

    def loop(low, high, step_of):
        def run(index, carry):
            step_of(index)
            return carry

        lax.fori_loop(low, high, run, 0)

    def swap(axis, count, mine, out_ref, in_ref, sems):
        def copy(step):
            return pltpu.make_async_remote_copy(
                src_ref=out_ref,
                dst_ref=in_ref.at[mine],
                send_sem=sems.at[0, step],
                recv_sem=sems.at[1, step],
                device_id={axis: lax.rem(mine + step, count)},
                device_id_type=MESH,
            )

        loop(1, count, lambda step: copy(step).start())
        in_ref[mine] = out_ref[...]
        return lambda: loop(1, count, lambda step: copy(step).wait())

    def start_stats(slot, first, second):
        stat_out[slot, 0] = first
        stat_out[slot, 1] = second
        wait = swap(
            "section", sections, me, stat_out.at[slot], stat_in.at[slot], stat_sems.at[slot]
        )

        def finish():
            wait()
            return jnp.sum(stat_in[slot], axis=0)

        return finish

    def weight_copies(step):
        peer = lax.rem(me + step, sections)
        lanes = pl.ds(pl.multiple_of(peer * chans, chans), chans)
        rows = pl.ds(pl.multiple_of(peer * group_rows, group_rows), group_rows)
        return [
            pltpu.make_async_remote_copy(
                src_ref=source,
                dst_ref=target,
                send_sem=weight_sems.at[0, kind, step],
                recv_sem=weight_sems.at[1, kind, step],
                device_id={"section": peer},
                device_id_type=MESH,
            )
            for kind, source, target in (
                (0, gs_hbm.at[:, lanes], gs_ref.at[me]),
                (1, taps_hbm.at[rows, :], taps_ref.at[me]),
            )
        ]

    def start_weights(step):
        for copy in weight_copies(step):
            copy.start()

    def wait_weights(step):
        for copy in weight_copies(step):
            copy.wait()

    own_rows = pl.ds(pl.multiple_of(me * group_rows, group_rows), group_rows)
    local_copies = [
        pltpu.make_async_copy(comp_ref.at[:, own_lanes], rows_in.at[0], local_sem.at[0]),
        pltpu.make_async_copy(gs_hbm.at[:, own_lanes], gs_ref.at[me], local_sem.at[1]),
        pltpu.make_async_copy(taps_hbm.at[own_rows, :], taps_ref.at[me], local_sem.at[2]),
    ]

    def pool_copy(section_step, resp_step):
        peer = lax.rem(me + section_step, sections)
        lanes = pl.ds(pl.multiple_of(peer * chans, chans), chans)
        return pltpu.make_async_remote_copy(
            src_ref=prompt_ref.at[:, lanes],
            dst_ref=pool.at[me, me_resp],
            send_sem=pool_send.at[section_step, resp_step],
            recv_sem=pool_recv.at[me, me_resp],
            device_id={"section": peer, "resp": lax.rem(me_resp + resp_step, n_resp)},
            device_id_type=MESH,
        )

    def pool_arrival(s, r):
        return pltpu.make_async_remote_copy(
            src_ref=prompt_ref.at[:, own_lanes],
            dst_ref=pool.at[s, r],
            send_sem=pool_send.at[0, 0],
            recv_sem=pool_recv.at[s, r],
            device_id={"section": lax.rem(me + 1, sections)},
            device_id_type=MESH,
        )

    own_pool = (
        pltpu.make_async_copy(
            prompt_ref.at[:, own_lanes], pool.at[me, me_resp], pool_recv.at[me, me_resp]
        )
        if direct
        else None
    )

    def pool_steps(action):
        def each(step):
            @pl.when(step > 0)
            def _():
                action(pool_copy(step // n_resp, step % n_resp))

        loop(0, sections * n_resp, each)

    def start_pool(s):
        @pl.when(me == s)
        def _():
            own_pool.start()
            pool_steps(lambda copy: copy.start())

    def wait_pool(s):
        def each(r):
            mine = (s == me) & (r == me_resp)

            @pl.when(mine)
            def _():
                own_pool.wait()

            @pl.when(jnp.logical_not(mine))
            def _():
                pool_arrival(s, r).wait_recv()

        loop(0, n_resp, each)

    for copy in local_copies:
        copy.start()
    loop(1, sections, start_weights)
    if direct:
        start_pool(0)
    for copy in local_copies:
        copy.wait()

    def first_stats(block):
        wide = rows_in[0, :, lane_slice(block)].astype(F32)
        stat_acc[...] += wide * wide

    stat_acc[...] = jnp.zeros_like(stat_acc)
    loop(0, blocks, first_stats)
    loop(1, sections, wait_weights)

    t_row = lax.broadcasted_iota(jnp.int32, (length, LANES), 0)
    s_lane = lax.broadcasted_iota(jnp.int32, (length, LANES), 1)
    keep = s_lane <= prompt_len + t_row
    s_row = lax.broadcasted_iota(jnp.int32, (total, LANES), 0)
    t_lane = lax.broadcasted_iota(jnp.int32, (total, LANES), 1)
    keep_t = s_row <= prompt_len + t_lane

    def build(s, block):
        rows = pl.ds(pl.multiple_of(block * groups, groups), groups)
        both = taps_ref[s, rows, :]
        flipped, plain = both[:, :LANES], both[:, LANES:]
        for g in range(groups):
            base = pl.multiple_of((block * groups + g) * length, length)
            wide = jnp.broadcast_to(flipped[g : g + 1], (length, LANES))
            wide = pltpu.roll(wide, prompt_len, 1, stride=1, stride_axis=0)
            wide = jnp.where(keep, wide, 0.0)
            high = wide.astype(BF16)
            low = (wide - high.astype(F32)).astype(BF16)
            toep[s, pl.ds(base, length), :] = jnp.concatenate([high, high, low], axis=1)
            base = pl.multiple_of((block * groups + g) * total, total)
            wide = jnp.broadcast_to(plain[g : g + 1], (total, LANES))
            wide = pltpu.roll(wide, prompt_len, 1, stride=1, stride_axis=0)
            toep_t[s, pl.ds(base, total), :] = jnp.where(keep_t, wide, 0.0).astype(BF16)

    def choose(s, block):
        lanes = lane_slice(block)
        for m in range(micro):
            rows = slice(m * prompt_len, (m + 1) * prompt_len)
            if direct:
                picked = jnp.zeros((prompt_len, LANES), F32)
                for r in range(n_resp):
                    flag = chosen_ref[m * n_resp + r : m * n_resp + r + 1, :] > 0.5
                    picked = jnp.where(flag, pool[s, r, :, lanes].astype(F32), picked)
                chosen_rows[s, rows, lanes] = picked.astype(BF16)
            else:
                picked = prompt_ref[s, rows, lanes].astype(F32)
                chosen_rows[s, rows, lanes] = prompt_ref[s, rows, lanes]
            prompt_acc[rows, :] += picked * picked

    row_id = lax.broadcasted_iota(jnp.int32, (total, LANES), 0)
    wide_group = (
        lax.broadcasted_iota(jnp.int32, (1, micro * LANES), 1) % LANES
    ) // per_group
    tap_count = gs_ref.shape[1] - 1

    def pick(stacked, rows):
        out = stacked[0:rows]
        for g in range(1, groups):
            out = jnp.where(wide_group == g, stacked[g * rows : (g + 1) * rows], out)
        return out

    def joined_rows(s, m, lanes):
        rows_p = slice(m * prompt_len, (m + 1) * prompt_len)
        rows_c = slice(m * length, (m + 1) * length)
        joined = jnp.concatenate(
            [chosen_rows[s, rows_p, lanes].astype(F32), rows_in[s, rows_c, lanes].astype(F32)],
            axis=0,
        )
        factor = jnp.concatenate([fac_p[s, rows_p, :], fac_c[s, rows_c, :]], axis=0)
        return joined, factor

    def forward(s, carry):
        if direct:
            wait_pool(s)
            start_pool(s + 1)
        prompt_acc[...] = jnp.zeros_like(prompt_acc)
        loop(0, blocks, lambda block: choose(s, block))
        finish = start_stats(s, rows_to_line(stat_acc[...]), rows_to_line(prompt_acc[...]))
        loop(0, blocks, lambda block: build(s, block))
        sums = finish()
        fac_c[s] = lax.rsqrt(line_to_rows(sums[0]) * (1.0 / width) + 1e-06)
        fac_p[s] = lax.rsqrt(line_to_rows(sums[1]) * (1.0 / width) + 1e-06)
        stat_acc[...] = jnp.zeros_like(stat_acc)
        score_acc[...] = jnp.zeros_like(score_acc)

        def run(block, carry):
            lanes = lane_slice(block)
            wide = wide_slice(block)
            gs = gs_ref[s, :, lanes]
            parts, lows, saved = [], [], []
            for m in range(micro):
                joined, factor = joined_rows(s, m, lanes)
                normed = joined * factor * gs[0:1]
                shorter = normed * gs[1:2]
                for j in range(1, tap_count):
                    moved = jnp.where(row_id >= j, pltpu.roll(normed, j, 0), 0.0)
                    shorter = shorter + moved * gs[1 + j : 2 + j]
                high = shorter.astype(BF16)
                parts.append(high)
                lows.append((shorter - high.astype(F32)).astype(BF16))
                saved.append((joined[prompt_len:], normed[prompt_len:]))
            high = jnp.concatenate(parts, axis=1)
            short_out[s, :, wide] = high
            rhs = jnp.concatenate([high, jnp.concatenate(lows, axis=1), high], axis=0)
            base = pl.multiple_of(block * groups * length, groups * length)
            stacked = jnp.dot(
                toep[s, pl.ds(base, groups * length), :], rhs, preferred_element_type=F32
            )
            longer_all = pick(stacked, length)
            for m in range(micro):
                rows = slice(m * length, (m + 1) * length)
                longer = longer_all[:, m * LANES : (m + 1) * LANES]
                long_out[s, rows, lanes] = longer
                mixed = (saved[m][0] + saved[m][1] * longer).astype(BF16)
                rows_in[s + 1, rows, lanes] = mixed
                mixed = mixed.astype(F32)
                stat_acc[rows, :] += mixed * mixed
                score_acc[rows, :] += mixed * head_ref[0:1, head_slice(block)]
            return carry

        lax.fori_loop(0, blocks, run, 0)

        return carry

    lax.fori_loop(0, sections, forward, 0)

    tile_rows = []
    for m in range(micro):
        rows = slice(m * length, (m + 1) * length)
        line = jnp.sum(score_acc[rows, :] * live_ref[rows, :], axis=0, keepdims=True)
        tile_rows.append(jnp.broadcast_to(jnp.sum(line, axis=1, keepdims=True), (1, LANES)))
    tile_rows.append(jnp.zeros((8 - micro, LANES), F32))
    score_tile = jnp.concatenate(tile_rows, axis=0)
    own_score = start_stats(sections, score_tile, score_tile)()[0]
    score_ref[...] = own_score
    resp_out[...] = own_score
    swap("resp", n_resp, me_resp, resp_out, resp_in, resp_sems)()
    margin = jnp.sum(resp_in[...] * pairs_ref[...], axis=0)
    weight = 1.0 / (1.0 + jnp.exp(margin))
    slopes = -jnp.sum(own_pairs_ref[...] * weight, axis=1, keepdims=True)

    def seed(block, carry):
        lanes = lane_slice(block)
        for m in range(micro):
            rows = slice(m * length, (m + 1) * length)
            upstream[rows, lanes] = live_ref[rows, :] * slopes[m : m + 1] * head_ref[0:1, head_slice(block)]
        return carry

    lax.fori_loop(0, blocks, seed, 0)

    keep_pair = total - 1 - s_lane <= prompt_len + t_row
    reverse = (
        lax.broadcasted_iota(jnp.int32, (total, total), 0)
        + lax.broadcasted_iota(jnp.int32, (total, total), 1)
        == total - 1
    )
    reverse = jnp.where(reverse, 1.0, 0.0).astype(BF16)

    share = 2 * blocks // n_resp

    def part_slice(r):
        return pl.ds(r * share, share)

    def part_steps(s, action):
        def each(step):
            peer = lax.rem(me_resp + step, n_resp)
            action(
                pltpu.make_async_remote_copy(
                    src_ref=tiles_own.at[s, part_slice(peer)],
                    dst_ref=tiles_in.at[s, me_resp],
                    send_sem=part_sems.at[0, s, step],
                    recv_sem=part_sems.at[1, s, step],
                    device_id={"resp": peer},
                    device_id_type=MESH,
                )
            )

        loop(1, n_resp, each)

    def tile_copy(s, step, k, r):
        return pltpu.make_async_remote_copy(
            src_ref=tiles_sum.at[s],
            dst_ref=tiles_ref.at[k, r],
            send_sem=tile_send.at[s, step],
            recv_sem=tile_recv.at[k, r],
            device_id={"section": s, "resp": lax.rem(me_resp + step, n_resp)},
            device_id_type=MESH,
        )

    def tile_steps(s, action):
        def each(step):
            @pl.when(jnp.logical_not((s == me) & (step == 0)))
            def _():
                action(tile_copy(s, step, me, me_resp))

        loop(0, n_resp, each)

    def backward(step, carry):
        s = sections - 1 - step
        stat_acc[...] = jnp.zeros_like(stat_acc)

        def run(block, carry):
            lanes = lane_slice(block)
            wide = wide_slice(block)
            gs = gs_ref[s, :, lanes]
            parts, saved = [], []
            for m in range(micro):
                rows = slice(m * length, (m + 1) * length)
                joined, factor = joined_rows(s, m, lanes)
                scaled = joined * factor
                normed = scaled * gs[0:1]
                above = upstream[rows, lanes]
                parts.append((above * normed[prompt_len:]).astype(BF16))
                saved.append((joined[prompt_len:], scaled, normed, above))
            d_long = jnp.concatenate(parts, axis=1)
            base = pl.multiple_of(block * groups * total, groups * total)
            stacked = jnp.dot(
                toep_t[s, pl.ds(base, groups * total), :][:, :length],
                d_long,
                preferred_element_type=F32,
            )
            d_short_all = pick(stacked, total)
            turned = jnp.dot(reverse, short_out[s, :, wide], preferred_element_type=F32)
            d_wide = d_long.astype(F32)
            masked = jnp.concatenate(
                [
                    jnp.where(wide_group == g, d_wide, 0.0).astype(BF16)
                    for g in range(groups)
                ],
                axis=0,
            )
            pairs = lax.dot_general(
                masked,
                turned.astype(BF16),
                (((1,), (1,)), ((), ())),
                preferred_element_type=F32,
            )
            lines = []
            for g in range(groups):
                one = jnp.where(keep_pair, pairs[g * length : (g + 1) * length], 0.0)
                one = pltpu.roll(one, LANES + 1 - length, 1, stride=1, stride_axis=0)
                lines.append(jnp.sum(one, axis=0, keepdims=True))
            tiles_own[s, 2 * block + 1] = jnp.concatenate(lines, axis=0)
            grads = [jnp.zeros((1, LANES), F32)] * (tap_count + 1)
            for m in range(micro):
                rows = slice(m * length, (m + 1) * length)
                joined_c, scaled, normed, above = saved[m]
                d_short = d_short_all[:, m * LANES : (m + 1) * LANES]
                d_normed = d_short * gs[1:2]
                grads[1] = grads[1] + jnp.sum(d_short * normed, axis=0, keepdims=True)
                for j in range(1, tap_count):
                    moved = jnp.where(
                        row_id < total - j, pltpu.roll(d_short, total - j, 0), 0.0
                    )
                    d_normed = d_normed + moved * gs[1 + j : 2 + j]
                    grads[1 + j] = grads[1 + j] + jnp.sum(
                        moved * normed, axis=0, keepdims=True
                    )
                direct = above * long_out[s, rows, lanes]
                d_normed = jnp.concatenate(
                    [d_normed[:prompt_len], d_normed[prompt_len:] + direct], axis=0
                )
                grads[0] = grads[0] + jnp.sum(d_normed * scaled, axis=0, keepdims=True)
                inner = d_normed[prompt_len:] * gs[0:1]
                partial[rows, lanes] = inner
                stat_acc[rows, :] += inner * joined_c
            tiles_own[s, 2 * block] = jnp.concatenate(grads, axis=0)
            return carry

        lax.fori_loop(0, blocks, run, 0)

        if direct:
            part_steps(s, lambda copy: copy.start())
            parts_in = tiles_in.at[s]
            parts_in[me_resp] = tiles_own[s, part_slice(me_resp)]

        @pl.when(s > 0)
        def _():
            line = rows_to_line(stat_acc[...])
            all_sums = start_stats(sections + 1 + step, line, line)()[0]
            factor = fac_c[s]
            pull = line_to_rows(all_sums) * (1.0 / width) * factor * factor * factor

            def finish(block, carry):
                lanes = lane_slice(block)
                grad = (
                    upstream[:, lanes]
                    + factor * partial[:, lanes]
                    - rows_in[s, :, lanes].astype(F32) * pull
                )
                upstream[:, lanes] = grad.astype(BF16).astype(F32)
                return carry

            lax.fori_loop(0, blocks, finish, 0)

        if direct:
            part_steps(s, lambda copy: copy.wait())
            tiles_sum[s] = jnp.sum(tiles_in[s], axis=0)

            @pl.when(s == me)
            def _():
                tiles_ref[me, me_resp] = tiles_sum[s]

            tile_steps(s, lambda copy: copy.start())

        return carry

    lax.fori_loop(0, sections, backward, 0)

    if direct:
        pool_steps(lambda copy: copy.wait_send())
        loop(0, sections, lambda s: tile_steps(s, lambda copy: copy.wait_send()))

        def arrive(step):
            k, r = step // n_resp, step % n_resp

            @pl.when(jnp.logical_not((k == me) & (r == me_resp)))
            def _():
                tile_copy(0, 0, k, r).wait_recv()

        loop(0, sections * n_resp, arrive)
    else:
        tiles_ref[...] = tiles_own[...]


def run_kernel(dims, direct, *arrays):
    sections, n_resp, micro, length, prompt_len, chans, per_group, width = dims
    rows = micro * length
    total = prompt_len + length
    group_total = chans // per_group
    tile = (8, LANES)
    tiles = 2 * chans // LANES
    share = tiles // n_resp if direct else 1
    ranks = n_resp if direct else 1
    vmem = pl.BlockSpec(memory_space=pltpu.VMEM)
    hbm = pl.BlockSpec(memory_space=pl.ANY)
    tiles_shape = (sections, n_resp, share) if direct else (sections, tiles)
    return pl.pallas_call(
        functools.partial(kernel, dims, direct),
        out_shape=(
            jax.ShapeDtypeStruct(tile, F32),
            jax.ShapeDtypeStruct(tiles_shape + tile, F32),
        ),
        in_specs=[hbm, hbm if direct else vmem, hbm, hbm] + [vmem] * (len(arrays) - 4),
        out_specs=(vmem,) * 2,
        scratch_shapes=[
            pltpu.VMEM((sections, group_total * length, 3 * LANES), BF16),
            pltpu.VMEM((sections, group_total * total, LANES), BF16),
            pltpu.VMEM((sections, ranks, prompt_len, chans), BF16),
            pltpu.VMEM((sections, micro * prompt_len, chans), BF16),
            pltpu.VMEM((sections, 8, chans), F32),
            pltpu.VMEM((sections, group_total, 2 * LANES), F32),
            pltpu.VMEM((sections + 1, rows, chans), BF16),
            pltpu.VMEM((sections, total, micro * chans), BF16),
            pltpu.VMEM((sections, rows, chans), F32),
            pltpu.VMEM((sections, micro * prompt_len, LANES), F32),
            pltpu.VMEM((sections, rows, LANES), F32),
            pltpu.VMEM((rows, chans), F32),
            pltpu.VMEM((rows, chans), F32),
            pltpu.VMEM((rows, LANES), F32),
            pltpu.VMEM((rows, LANES), F32),
            pltpu.VMEM((micro * prompt_len, LANES), F32),
            pltpu.VMEM((2 * sections, 2) + tile, F32),
            pltpu.VMEM((2 * sections, sections, 2) + tile, F32),
            pltpu.VMEM(tile, F32),
            pltpu.VMEM((n_resp,) + tile, F32),
            pltpu.VMEM((sections, tiles) + tile, F32),
            pltpu.VMEM((sections, ranks, share) + tile, F32),
            pltpu.VMEM((sections, share) + tile, F32),
            pltpu.SemaphoreType.DMA((3,)),
            pltpu.SemaphoreType.DMA((2, 2, sections)),
            pltpu.SemaphoreType.DMA((sections, ranks)),
            pltpu.SemaphoreType.DMA((sections, ranks)),
            pltpu.SemaphoreType.DMA((2 * sections, 2, sections)),
            pltpu.SemaphoreType.DMA((2, n_resp)),
            pltpu.SemaphoreType.DMA((2, sections, ranks)),
            pltpu.SemaphoreType.DMA((sections, ranks)),
            pltpu.SemaphoreType.DMA((sections, ranks)),
        ],
        compiler_params=pltpu.CompilerParams(
            has_side_effects=True, vmem_limit_bytes=56 * 1024 * 1024
        ),
    )(*arrays)


def body(
    completion_rows,
    prompt_pool,
    norm_gain,
    short_taps,
    long_taps,
    score_head,
    live_lengths,
    prompt_owner,
    pair_index,
):
    sections = lax.axis_size("section")
    n_resp = lax.axis_size("resp")
    me_resp = lax.axis_index("resp")
    micro, _, length, width = completion_rows.shape
    prompt_len = prompt_pool.shape[2]
    chans = width // sections
    tap_len, group_all = long_taps.shape[1:]
    per_group = width // group_all
    dims = (sections, n_resp, micro, length, prompt_len, chans, per_group, width)

    tiles = 2 * chans // LANES
    direct = n_resp <= 8 and tiles % n_resp == 0

    gs = jnp.concatenate([norm_gain, short_taps[0]], axis=0)
    taps = long_taps[0].T
    flipped = jnp.concatenate([taps[:, :1], taps[:, :0:-1]], axis=1)
    taps = jnp.concatenate([flipped, taps], axis=1)
    prompts = prompt_pool[0, 0]
    mine = prompt_owner[:, None] == jnp.arange(n_resp, dtype=jnp.int32)[None]
    chosen = jnp.broadcast_to(
        mine.astype(F32).reshape(micro * n_resp, 1), (micro * n_resp, LANES)
    )
    if not direct:
        split = prompts.reshape(prompt_len, sections, chans).transpose(1, 0, 2)
        split = lax.all_to_all(split, "section", 0, 0, tiled=True)
        here = (prompt_owner == me_resp)[None, :, None, None]
        split = lax.psum(jnp.where(here, split[:, None], jnp.zeros((), BF16)), "resp")
        prompts = split.reshape(sections, micro * prompt_len, chans)
    rows = completion_rows.reshape(micro * length, width)
    head = score_head[None]

    labels = jnp.arange(n_resp, dtype=jnp.int32)[:, None, None]
    ends = (pair_index[None, :, :, 0] == labels).astype(F32) - (
        pair_index[None, :, :, 1] == labels
    ).astype(F32)
    pairs = jnp.pad(ends, ((0, 0), (0, 8 - micro), (0, LANES - ends.shape[2])))
    own_pairs = lax.dynamic_index_in_dim(pairs, me_resp, 0, keepdims=False)
    lengths = live_lengths[:, 0]
    live = (jnp.arange(length, dtype=jnp.int32)[None] < lengths[:, None]).astype(F32)
    live = (live / jnp.sqrt(lengths.astype(F32))[:, None]).reshape(micro * length, 1)
    live = jnp.broadcast_to(live, (micro * length, LANES))

    scores, grads = run_kernel(
        dims, direct, rows, prompts, gs, taps, chosen, head, pairs, own_pairs, live
    )
    if not direct:
        grads = lax.psum(grads, "resp")
        grads = lax.all_to_all(grads, "section", 0, 0, tiled=True)
    grads = grads.reshape(sections * tiles // 2, 2, 8, LANES)
    gs_grad = grads[:, 0].transpose(1, 0, 2).reshape(8, width)
    taps_grad = grads[:, 1].reshape(group_all, tap_len).T
    return (
        scores[:micro, :1].astype(BF16),
        gs_grad[:1],
        gs_grad[None, 1:],
        taps_grad[None],
    )


def solution(mesh):
    placed = (
        P(None, ("groups", "resp"), None, None),
        P("section", ("groups", "resp"), None, None),
        P("section", None),
        P("section", None, None),
        P("section", None, None),
        P(),
        P(None, ("groups", "resp")),
        P("groups"),
        P(None, "groups", None),
    )
    return jax.shard_map(
        body,
        mesh=mesh,
        in_specs=placed,
        out_specs=(
            P(None, ("groups", "resp")),
            P("section", "groups"),
            P("section", "groups", None),
            P("section", "groups", None),
        ),
        check_vma=False,
    )
```

```python
import functools

import jax
import jax.numpy as jnp
from jax import lax
from jax.experimental import pallas as pl
from jax.experimental.pallas import tpu as pltpu
from jax.sharding import PartitionSpec as P

LANES = 128
MESH = pl.DeviceIdType.MESH
F32 = jnp.float32
BF16 = jnp.bfloat16


def rows_to_line(block):
    line = jnp.sum(jnp.transpose(block), axis=0, keepdims=True)
    return jnp.broadcast_to(line, (8, LANES))


def line_to_rows(tile):
    return jnp.transpose(jnp.broadcast_to(tile[0:1], (LANES, LANES)))


def kernel(
    dims,
    direct,
    comp_ref,
    prompt_ref,
    gain_hbm,
    short_hbm,
    taps_hbm,
    owner_ref,
    head_ref,
    ends_ref,
    length_ref,
    score_ref,
    *rest,
):
    sections, n_resp, micro, length, prompt_len, chans, per_group, width = dims
    outs, rest = (rest[:3], rest[3:]) if direct else (rest[:1], rest[1:])
    (
        toep,
        toep_t,
        pool,
        chosen_rows,
        gain_ref,
        short_ref,
        taps_ref,
        rows_in,
        short_out,
        long_out,
        fac_p,
        fac_c,
        upstream,
        partial,
        stat_acc,
        score_acc,
        prompt_acc,
        stat_out,
        stat_in,
        resp_out,
        resp_in,
        tiles_own,
        tiles_in,
        tiles_sum,
        tiles_all,
        local_sem,
        weight_sems,
        spread_sems,
        pool_sems,
        stat_sems,
        resp_sems,
        part_sems,
        tile_send,
        tile_recv,
    ) = rest
    groups = LANES // per_group
    blocks = chans // LANES
    group_rows = blocks * groups
    total = prompt_len + length
    me = lax.axis_index("section")
    me_resp = lax.axis_index("resp")
    own_lanes = pl.ds(pl.multiple_of(me * chans, chans), chans)

    def lane_slice(block):
        return pl.ds(pl.multiple_of(block * LANES, LANES), LANES)

    def head_slice(block):
        return pl.ds(pl.multiple_of(me * chans + block * LANES, LANES), LANES)

    def wide_slice(block):
        return pl.ds(pl.multiple_of(block * micro * LANES, LANES), micro * LANES)

    def loop(low, high, step_of):
        def run(index, carry):
            step_of(index)
            return carry

        lax.fori_loop(low, high, run, 0)

    def swap(axis, count, mine, out_ref, in_ref, sems):
        def copy(step):
            return pltpu.make_async_remote_copy(
                src_ref=out_ref,
                dst_ref=in_ref.at[mine],
                send_sem=sems.at[0, step],
                recv_sem=sems.at[1, step],
                device_id={axis: lax.rem(mine + step, count)},
                device_id_type=MESH,
            )

        loop(1, count, lambda step: copy(step).start())
        in_ref[mine] = out_ref[...]
        return lambda: loop(1, count, lambda step: copy(step).wait())

    def start_stats(slot, first, second):
        stat_out[slot, 0] = first
        stat_out[slot, 1] = second
        wait = swap(
            "section", sections, me, stat_out.at[slot], stat_in.at[slot], stat_sems.at[slot]
        )

        def finish():
            wait()
            return jnp.sum(stat_in[slot], axis=0)

        return finish

    def weight_copies(step):
        peer = lax.rem(me + step, sections)
        lanes = pl.ds(pl.multiple_of(peer * chans, chans), chans)
        rows = pl.ds(pl.multiple_of(peer * group_rows, group_rows), group_rows)
        return [
            pltpu.make_async_remote_copy(
                src_ref=source,
                dst_ref=target,
                send_sem=weight_sems.at[0, kind, step],
                recv_sem=weight_sems.at[1, kind, step],
                device_id={"section": peer},
                device_id_type=MESH,
            )
            for kind, source, target in (
                (0, gain_hbm.at[:, lanes], gain_ref.at[me]),
                (2, short_hbm.at[:, lanes], short_ref.at[me]),
                (1, taps_hbm.at[rows, :], taps_ref.at[me]),
            )
        ]

    def start_weights(step):
        for copy in weight_copies(step):
            copy.start()

    def wait_weights(step):
        for copy in weight_copies(step):
            copy.wait()

    own_rows = pl.ds(pl.multiple_of(me * group_rows, group_rows), group_rows)
    local_copies = [
        pltpu.make_async_copy(comp_ref.at[:, own_lanes], rows_in.at[0], local_sem.at[0]),
        pltpu.make_async_copy(gain_hbm.at[:, own_lanes], gain_ref.at[me], local_sem.at[1]),
        pltpu.make_async_copy(short_hbm.at[:, own_lanes], short_ref.at[me], local_sem.at[3]),
        pltpu.make_async_copy(taps_hbm.at[own_rows, :], taps_ref.at[me], local_sem.at[2]),
    ]

    def spread_copy(step):
        peer = lax.rem(me + step, sections)
        lanes = pl.ds(pl.multiple_of(peer * chans, chans), chans)
        return pltpu.make_async_remote_copy(
            src_ref=prompt_ref.at[:, lanes],
            dst_ref=pool.at[me, me_resp],
            send_sem=spread_sems.at[0, step],
            recv_sem=spread_sems.at[1, step],
            device_id={"section": peer},
            device_id_type=MESH,
        )

    def pool_copy(s, step):
        return pltpu.make_async_remote_copy(
            src_ref=pool.at[s, me_resp],
            dst_ref=pool.at[s, me_resp],
            send_sem=pool_sems.at[0, s, step],
            recv_sem=pool_sems.at[1, s, step],
            device_id={"resp": lax.rem(me_resp + step, n_resp)},
            device_id_type=MESH,
        )

    def own_pool():
        return pltpu.make_async_copy(
            prompt_ref.at[:, own_lanes], pool.at[me, me_resp], local_sem.at[4]
        )

    def start_pool(s):
        step = lax.rem(me - s + sections, sections)

        @pl.when(step == 0)
        def _():
            own_pool().wait()

        @pl.when(step > 0)
        def _():
            spread_copy(step).wait()

        loop(1, n_resp, lambda d: pool_copy(s, d).start())

    def wait_pool(s):
        loop(1, n_resp, lambda d: pool_copy(s, d).wait())

    if direct:
        own_pool().start()
        loop(1, sections, lambda step: spread_copy(step).start())
    for copy in local_copies:
        copy.start()
    loop(1, sections, start_weights)
    if direct:
        start_pool(0)
    for copy in local_copies:
        copy.wait()

    def first_stats(block):
        wide = rows_in[0, :, lane_slice(block)].astype(F32)
        stat_acc[...] += wide * wide

    stat_acc[...] = jnp.zeros_like(stat_acc)
    loop(0, blocks, first_stats)
    loop(1, sections, wait_weights)

    t_row = lax.broadcasted_iota(jnp.int32, (length, LANES), 0)
    s_lane = lax.broadcasted_iota(jnp.int32, (length, LANES), 1)
    keep = s_lane <= prompt_len + t_row
    s_row = lax.broadcasted_iota(jnp.int32, (total, LANES), 0)
    t_lane = lax.broadcasted_iota(jnp.int32, (total, LANES), 1)
    keep_t = s_row <= prompt_len + t_lane

    def build(s, block):
        rows = pl.ds(pl.multiple_of(block * groups, groups), groups)
        both = taps_ref[s, rows, :]
        flipped, plain = both[:, :LANES], both[:, LANES:]
        for g in range(groups):
            base = pl.multiple_of((block * groups + g) * length, length)
            wide = jnp.broadcast_to(flipped[g : g + 1], (length, LANES))
            wide = pltpu.roll(wide, prompt_len, 1, stride=1, stride_axis=0)
            wide = jnp.where(keep, wide, 0.0)
            high = wide.astype(BF16)
            low = (wide - high.astype(F32)).astype(BF16)
            toep[s, pl.ds(base, length), :] = jnp.concatenate([high, high, low], axis=1)
            base = pl.multiple_of((block * groups + g) * total, total)
            wide = jnp.broadcast_to(plain[g : g + 1], (total, LANES))
            wide = pltpu.roll(wide, prompt_len, 1, stride=1, stride_axis=0)
            toep_t[s, pl.ds(base, total), :] = jnp.where(keep_t, wide, 0.0).astype(BF16)

    def choose(s, block):
        lanes = lane_slice(block)
        for m in range(micro):
            rows = slice(m * prompt_len, (m + 1) * prompt_len)
            if direct:
                picked = jnp.zeros((prompt_len, LANES), F32)
                for r in range(n_resp):
                    flag = jnp.full((prompt_len, LANES), owner_ref[m], jnp.int32) == r
                    picked = jnp.where(flag, pool[s, r, :, lanes].astype(F32), picked)
                chosen_rows[s, rows, lanes] = picked.astype(BF16)
            else:
                picked = prompt_ref[s, rows, lanes].astype(F32)
                chosen_rows[s, rows, lanes] = prompt_ref[s, rows, lanes]
            prompt_acc[rows, :] += picked * picked

    row_id = lax.broadcasted_iota(jnp.int32, (total, LANES), 0)
    wide_group = (
        lax.broadcasted_iota(jnp.int32, (1, micro * LANES), 1) % LANES
    ) // per_group
    tap_count = short_ref.shape[1]

    def pick(stacked, rows):
        out = stacked[0:rows]
        for g in range(1, groups):
            out = jnp.where(wide_group == g, stacked[g * rows : (g + 1) * rows], out)
        return out

    def joined_rows(s, m, lanes):
        rows_p = slice(m * prompt_len, (m + 1) * prompt_len)
        rows_c = slice(m * length, (m + 1) * length)
        joined = jnp.concatenate(
            [chosen_rows[s, rows_p, lanes].astype(F32), rows_in[s, rows_c, lanes].astype(F32)],
            axis=0,
        )
        factor = jnp.concatenate([fac_p[s, rows_p, :], fac_c[s, rows_c, :]], axis=0)
        return joined, factor

    def forward(s, carry):
        if direct:
            wait_pool(s)

            @pl.when(s + 1 < sections)
            def _():
                start_pool(s + 1)

        prompt_acc[...] = jnp.zeros_like(prompt_acc)
        loop(0, blocks, lambda block: choose(s, block))
        finish = start_stats(s, rows_to_line(stat_acc[...]), rows_to_line(prompt_acc[...]))
        loop(0, blocks, lambda block: build(s, block))
        sums = finish()
        fac_c[s] = lax.rsqrt(line_to_rows(sums[0]) * (1.0 / width) + 1e-06)
        fac_p[s] = lax.rsqrt(line_to_rows(sums[1]) * (1.0 / width) + 1e-06)
        stat_acc[...] = jnp.zeros_like(stat_acc)
        score_acc[...] = jnp.zeros_like(score_acc)

        def run(block, carry):
            lanes = lane_slice(block)
            wide = wide_slice(block)
            gain = gain_ref[s, :, lanes]
            short = short_ref[s, :, lanes]
            parts, lows, saved = [], [], []
            for m in range(micro):
                joined, factor = joined_rows(s, m, lanes)
                normed = joined * factor * gain
                shorter = normed * short[0:1]
                for j in range(1, tap_count):
                    moved = jnp.where(row_id >= j, pltpu.roll(normed, j, 0), 0.0)
                    shorter = shorter + moved * short[j : j + 1]
                high = shorter.astype(BF16)
                parts.append(high)
                lows.append((shorter - high.astype(F32)).astype(BF16))
                saved.append((joined[prompt_len:], normed[prompt_len:]))
            high = jnp.concatenate(parts, axis=1)
            short_out[s, :, wide] = high
            rhs = jnp.concatenate([high, jnp.concatenate(lows, axis=1), high], axis=0)
            base = pl.multiple_of(block * groups * length, groups * length)
            stacked = jnp.dot(
                toep[s, pl.ds(base, groups * length), :], rhs, preferred_element_type=F32
            )
            longer_all = pick(stacked, length)
            for m in range(micro):
                rows = slice(m * length, (m + 1) * length)
                longer = longer_all[:, m * LANES : (m + 1) * LANES]
                long_out[s, rows, lanes] = longer
                mixed = (saved[m][0] + saved[m][1] * longer).astype(BF16)
                rows_in[s + 1, rows, lanes] = mixed
                mixed = mixed.astype(F32)
                stat_acc[rows, :] += mixed * mixed
                score_acc[rows, :] += mixed * head_ref[0:1, head_slice(block)]
            return carry

        lax.fori_loop(0, blocks, run, 0)

        return carry

    lax.fori_loop(0, sections, forward, 0)

    live = []
    for m in range(micro):
        count = jnp.full((length, LANES), length_ref[m, 0], jnp.int32)
        live.append(jnp.where(t_row < count, 1.0, 0.0) / jnp.sqrt(count.astype(F32)))
    tile_rows = []
    for m in range(micro):
        rows = slice(m * length, (m + 1) * length)
        line = jnp.sum(score_acc[rows, :] * live[m], axis=0, keepdims=True)
        tile_rows.append(jnp.broadcast_to(jnp.sum(line, axis=1, keepdims=True), (1, LANES)))
    tile_rows.append(jnp.zeros((8 - micro, LANES), F32))
    score_tile = jnp.concatenate(tile_rows, axis=0)
    own_score = start_stats(sections, score_tile, score_tile)()[0]
    score_ref[...] = own_score
    resp_out[...] = own_score
    swap("resp", n_resp, me_resp, resp_out, resp_in, resp_sems)()
    winner, loser = ends_ref[0], ends_ref[1]

    def signs(r):
        return jnp.where(winner == r, 1.0, 0.0) - jnp.where(loser == r, 1.0, 0.0)

    margin = lax.fori_loop(
        0, n_resp, lambda r, acc: acc + resp_in[r] * signs(r), jnp.zeros((8, LANES), F32)
    )
    weight = 1.0 / (1.0 + jnp.exp(margin))
    slopes = -jnp.sum(signs(me_resp) * weight, axis=1, keepdims=True)

    def seed(block, carry):
        lanes = lane_slice(block)
        for m in range(micro):
            rows = slice(m * length, (m + 1) * length)
            upstream[rows, lanes] = live[m] * slopes[m : m + 1] * head_ref[0:1, head_slice(block)]
        return carry

    lax.fori_loop(0, blocks, seed, 0)

    keep_pair = total - 1 - s_lane <= prompt_len + t_row
    reverse = (
        lax.broadcasted_iota(jnp.int32, (total, total), 0)
        + lax.broadcasted_iota(jnp.int32, (total, total), 1)
        == total - 1
    )
    reverse = jnp.where(reverse, 1.0, 0.0).astype(BF16)

    share = 2 * blocks // n_resp

    def part_slice(r):
        return pl.ds(r * share, share)

    def part_steps(s, action):
        def each(step):
            peer = lax.rem(me_resp + step, n_resp)
            action(
                pltpu.make_async_remote_copy(
                    src_ref=tiles_own.at[s, part_slice(peer)],
                    dst_ref=tiles_in.at[s, me_resp],
                    send_sem=part_sems.at[0, s, step],
                    recv_sem=part_sems.at[1, s, step],
                    device_id={"resp": peer},
                    device_id_type=MESH,
                )
            )

        loop(1, n_resp, each)

    def tile_copy(s, step, k, r):
        return pltpu.make_async_remote_copy(
            src_ref=tiles_sum.at[s],
            dst_ref=tiles_all.at[k, r],
            send_sem=tile_send.at[s, step],
            recv_sem=tile_recv.at[k, r],
            device_id={"section": s, "resp": lax.rem(me_resp + step, n_resp)},
            device_id_type=MESH,
        )

    def tile_steps(s, action):
        def each(step):
            @pl.when(jnp.logical_not((s == me) & (step == 0)))
            def _():
                action(tile_copy(s, step, me, me_resp))

        loop(0, n_resp, each)

    def backward(step, carry):
        s = sections - 1 - step
        stat_acc[...] = jnp.zeros_like(stat_acc)

        def run(block, carry):
            lanes = lane_slice(block)
            wide = wide_slice(block)
            gain = gain_ref[s, :, lanes]
            short = short_ref[s, :, lanes]
            parts, saved = [], []
            for m in range(micro):
                rows = slice(m * length, (m + 1) * length)
                joined, factor = joined_rows(s, m, lanes)
                scaled = joined * factor
                normed = scaled * gain
                above = upstream[rows, lanes]
                parts.append((above * normed[prompt_len:]).astype(BF16))
                saved.append((joined[prompt_len:], scaled, normed, above))
            d_long = jnp.concatenate(parts, axis=1)
            base = pl.multiple_of(block * groups * total, groups * total)
            stacked = jnp.dot(
                toep_t[s, pl.ds(base, groups * total), :][:, :length],
                d_long,
                preferred_element_type=F32,
            )
            d_short_all = pick(stacked, total)
            turned = jnp.dot(reverse, short_out[s, :, wide], preferred_element_type=F32)
            d_wide = d_long.astype(F32)
            masked = jnp.concatenate(
                [
                    jnp.where(wide_group == g, d_wide, 0.0).astype(BF16)
                    for g in range(groups)
                ],
                axis=0,
            )
            pairs = lax.dot_general(
                masked,
                turned.astype(BF16),
                (((1,), (1,)), ((), ())),
                preferred_element_type=F32,
            )
            lines = []
            for g in range(groups):
                one = jnp.where(keep_pair, pairs[g * length : (g + 1) * length], 0.0)
                one = pltpu.roll(one, LANES + 1 - length, 1, stride=1, stride_axis=0)
                lines.append(jnp.sum(one, axis=0, keepdims=True))
            tiles_own[s, 2 * block + 1] = jnp.concatenate(lines, axis=0)
            grads = [jnp.zeros((1, LANES), F32)] * (tap_count + 1)
            for m in range(micro):
                rows = slice(m * length, (m + 1) * length)
                joined_c, scaled, normed, above = saved[m]
                d_short = d_short_all[:, m * LANES : (m + 1) * LANES]
                d_normed = d_short * short[0:1]
                grads[1] = grads[1] + jnp.sum(d_short * normed, axis=0, keepdims=True)
                for j in range(1, tap_count):
                    moved = jnp.where(
                        row_id < total - j, pltpu.roll(d_short, total - j, 0), 0.0
                    )
                    d_normed = d_normed + moved * short[j : j + 1]
                    grads[1 + j] = grads[1 + j] + jnp.sum(
                        moved * normed, axis=0, keepdims=True
                    )
                direct = above * long_out[s, rows, lanes]
                d_normed = jnp.concatenate(
                    [d_normed[:prompt_len], d_normed[prompt_len:] + direct], axis=0
                )
                grads[0] = grads[0] + jnp.sum(d_normed * scaled, axis=0, keepdims=True)
                inner = d_normed[prompt_len:] * gain
                partial[rows, lanes] = inner
                stat_acc[rows, :] += inner * joined_c
            tiles_own[s, 2 * block] = jnp.concatenate(grads, axis=0)
            return carry

        lax.fori_loop(0, blocks, run, 0)

        if direct:
            part_steps(s, lambda copy: copy.start())
            parts_in = tiles_in.at[s]
            parts_in[me_resp] = tiles_own[s, part_slice(me_resp)]

        @pl.when(s > 0)
        def _():
            line = rows_to_line(stat_acc[...])
            all_sums = start_stats(sections + 1 + step, line, line)()[0]
            factor = fac_c[s]
            pull = line_to_rows(all_sums) * (1.0 / width) * factor * factor * factor

            def finish(block, carry):
                lanes = lane_slice(block)
                grad = (
                    upstream[:, lanes]
                    + factor * partial[:, lanes]
                    - rows_in[s, :, lanes].astype(F32) * pull
                )
                upstream[:, lanes] = grad.astype(BF16).astype(F32)
                return carry

            lax.fori_loop(0, blocks, finish, 0)

        if direct:
            part_steps(s, lambda copy: copy.wait())
            tiles_sum[s] = jnp.sum(tiles_in[s], axis=0)

            @pl.when(s == me)
            def _():
                tiles_all[me, me_resp] = tiles_sum[s]

            tile_steps(s, lambda copy: copy.start())

        return carry

    lax.fori_loop(0, sections, backward, 0)

    if direct:
        loop(0, sections, lambda s: tile_steps(s, lambda copy: copy.wait_send()))

        def arrive(step):
            k, r = step // n_resp, step % n_resp

            @pl.when(jnp.logical_not((k == me) & (r == me_resp)))
            def _():
                tile_copy(0, 0, k, r).wait_recv()

        loop(0, sections * n_resp, arrive)
        gain_out, taps_short_out, taps_long_out = outs
        per_line = LANES // groups
        for line in range(sections * blocks // per_line):
            lines = []
            for place in range(per_line):
                block = line * per_line + place
                lanes = slice(block * LANES, (block + 1) * LANES)
                owner, local = divmod(2 * block, 2 * blocks)
                first, second = (divmod(local + kind, share) for kind in range(2))
                tile = tiles_all[owner, first[0], first[1]]
                gain_out[:, lanes] = tile[0:1]
                taps_short_out[:, lanes] = tile[1:]
                lines.append(tiles_all[owner, second[0], second[1]])
            lanes = slice(line * LANES, (line + 1) * LANES)
            taps_long_out[:, lanes] = jnp.transpose(jnp.concatenate(lines, axis=0))
    else:
        outs[0][...] = tiles_own[...]


def run_kernel(dims, direct, *arrays):
    sections, n_resp, micro, length, prompt_len, chans, per_group, width = dims
    rows = micro * length
    total = prompt_len + length
    group_total = chans // per_group
    tile = (8, LANES)
    tiles = 2 * chans // LANES
    share = tiles // n_resp if direct else 1
    ranks = n_resp if direct else 1
    vmem = pl.BlockSpec(memory_space=pltpu.VMEM)
    hbm = pl.BlockSpec(memory_space=pl.ANY)
    smem = pl.BlockSpec(memory_space=pltpu.SMEM)
    tap_count = arrays[3].shape[0]
    if direct:
        out_shapes = [(1, width), (tap_count, width), (LANES, width // per_group)]
    else:
        out_shapes = [(sections, tiles) + tile]
    return pl.pallas_call(
        functools.partial(kernel, dims, direct),
        out_shape=(
            jax.ShapeDtypeStruct(tile, F32),
            *(jax.ShapeDtypeStruct(shape, F32) for shape in out_shapes),
        ),
        in_specs=[hbm, hbm if direct else vmem, hbm, hbm, hbm, smem, vmem, vmem, smem],
        out_specs=(vmem,) * (1 + len(out_shapes)),
        scratch_shapes=[
            pltpu.VMEM((sections, group_total * length, 3 * LANES), BF16),
            pltpu.VMEM((sections, group_total * total, LANES), BF16),
            pltpu.VMEM((sections, ranks, prompt_len, chans), BF16),
            pltpu.VMEM((sections, micro * prompt_len, chans), BF16),
            pltpu.VMEM((sections, 1, chans), F32),
            pltpu.VMEM((sections, tap_count, chans), F32),
            pltpu.VMEM((sections, group_total, 2 * LANES), F32),
            pltpu.VMEM((sections + 1, rows, chans), BF16),
            pltpu.VMEM((sections, total, micro * chans), BF16),
            pltpu.VMEM((sections, rows, chans), F32),
            pltpu.VMEM((sections, micro * prompt_len, LANES), F32),
            pltpu.VMEM((sections, rows, LANES), F32),
            pltpu.VMEM((rows, chans), F32),
            pltpu.VMEM((rows, chans), F32),
            pltpu.VMEM((rows, LANES), F32),
            pltpu.VMEM((rows, LANES), F32),
            pltpu.VMEM((micro * prompt_len, LANES), F32),
            pltpu.VMEM((2 * sections, 2) + tile, F32),
            pltpu.VMEM((2 * sections, sections, 2) + tile, F32),
            pltpu.VMEM(tile, F32),
            pltpu.VMEM((n_resp,) + tile, F32),
            pltpu.VMEM((sections, tiles) + tile, F32),
            pltpu.VMEM((sections, ranks, share) + tile, F32),
            pltpu.VMEM((sections, share) + tile, F32),
            pltpu.VMEM((sections, ranks, share) + tile, F32),
            pltpu.SemaphoreType.DMA((5,)),
            pltpu.SemaphoreType.DMA((2, 3, sections)),
            pltpu.SemaphoreType.DMA((2, sections)),
            pltpu.SemaphoreType.DMA((2, sections, ranks)),
            pltpu.SemaphoreType.DMA((2 * sections, 2, sections)),
            pltpu.SemaphoreType.DMA((2, n_resp)),
            pltpu.SemaphoreType.DMA((2, sections, ranks)),
            pltpu.SemaphoreType.DMA((sections, ranks)),
            pltpu.SemaphoreType.DMA((sections, ranks)),
        ],
        compiler_params=pltpu.CompilerParams(
            has_side_effects=True, vmem_limit_bytes=56 * 1024 * 1024
        ),
    )(*arrays)


def body(
    completion_rows,
    prompt_pool,
    norm_gain,
    short_taps,
    long_taps,
    score_head,
    live_lengths,
    prompt_owner,
    pair_index,
):
    sections = lax.axis_size("section")
    n_resp = lax.axis_size("resp")
    me_resp = lax.axis_index("resp")
    micro, _, length, width = completion_rows.shape
    prompt_len = prompt_pool.shape[2]
    chans = width // sections
    tap_len, group_all = long_taps.shape[1:]
    per_group = width // group_all
    dims = (sections, n_resp, micro, length, prompt_len, chans, per_group, width)

    tiles = 2 * chans // LANES
    direct = n_resp <= 8 and tiles % n_resp == 0

    taps = long_taps[0].T
    flipped = jnp.concatenate([taps[:, :1], taps[:, :0:-1]], axis=1)
    taps = jnp.concatenate([flipped, taps], axis=1)
    prompts = prompt_pool[0, 0]
    if not direct:
        split = prompts.reshape(prompt_len, sections, chans).transpose(1, 0, 2)
        split = lax.all_to_all(split, "section", 0, 0, tiled=True)
        here = (prompt_owner == me_resp)[None, :, None, None]
        split = lax.psum(jnp.where(here, split[:, None], jnp.zeros((), BF16)), "resp")
        prompts = split.reshape(sections, micro * prompt_len, chans)
    rows = completion_rows.reshape(micro * length, width)
    head = score_head[None]

    ends = jnp.pad(
        pair_index.transpose(2, 0, 1),
        ((0, 0), (0, 8 - micro), (0, LANES - pair_index.shape[1])),
        constant_values=-1,
    )
    scores, *grads = run_kernel(
        dims,
        direct,
        rows,
        prompts,
        norm_gain,
        short_taps[0],
        taps,
        prompt_owner,
        head,
        ends,
        live_lengths,
    )
    scores = scores[:micro, :1].astype(BF16)
    if direct:
        return (scores, grads[0], grads[1][None], grads[2][None])
    grads = lax.psum(grads[0], "resp")
    grads = lax.all_to_all(grads, "section", 0, 0, tiled=True)
    grads = grads.reshape(sections * tiles // 2, 2, 8, LANES)
    gs_grad = grads[:, 0].transpose(1, 0, 2).reshape(8, width)
    taps_grad = grads[:, 1].reshape(group_all, tap_len).T
    return (
        scores,
        gs_grad[:1],
        gs_grad[None, 1:],
        taps_grad[None],
    )


def solution(mesh):
    placed = (
        P(None, ("groups", "resp"), None, None),
        P("section", ("groups", "resp"), None, None),
        P("section", None),
        P("section", None, None),
        P("section", None, None),
        P(),
        P(None, ("groups", "resp")),
        P("groups"),
        P(None, "groups", None),
    )
    return jax.shard_map(
        body,
        mesh=mesh,
        in_specs=placed,
        out_specs=(
            P(None, ("groups", "resp")),
            P("section", "groups"),
            P("section", "groups", None),
            P("section", "groups", None),
        ),
        check_vma=False,
    )
```

```python
import functools

import jax
import jax.numpy as jnp
from jax import lax
from jax.experimental import pallas as pl
from jax.experimental.pallas import tpu as pltpu
from jax.sharding import PartitionSpec as P

LANES = 128
MESH = pl.DeviceIdType.MESH
F32 = jnp.float32
BF16 = jnp.bfloat16


def rows_to_line(block):
    line = jnp.sum(jnp.transpose(block), axis=0, keepdims=True)
    return jnp.broadcast_to(line, (8, LANES))


def line_to_rows(tile):
    return jnp.transpose(jnp.broadcast_to(tile[0:1], (LANES, LANES)))


def kernel(
    dims,
    direct,
    comp_ref,
    prompt_ref,
    gain_hbm,
    short_hbm,
    taps_hbm,
    owner_ref,
    head_ref,
    ends_ref,
    length_ref,
    score_ref,
    *rest,
):
    sections, n_resp, micro, length, prompt_len, chans, per_group, width = dims
    outs, rest = (rest[:3], rest[3:]) if direct else (rest[:1], rest[1:])
    (
        toep,
        toep_t,
        pool,
        chosen_rows,
        gain_ref,
        short_ref,
        taps_ref,
        rows_in,
        short_out,
        long_out,
        fac_p,
        fac_c,
        upstream,
        partial,
        stat_acc,
        score_acc,
        prompt_acc,
        stat_out,
        stat_in,
        resp_out,
        resp_in,
        tiles_own,
        tiles_in,
        tiles_sum,
        tiles_all,
        local_sem,
        weight_sems,
        spread_sems,
        pool_sems,
        stat_sems,
        resp_sems,
        part_sems,
        tile_send,
        tile_recv,
    ) = rest
    groups = LANES // per_group
    blocks = chans // LANES
    group_rows = blocks * groups
    total = prompt_len + length
    me = lax.axis_index("section")
    me_resp = lax.axis_index("resp")
    own_lanes = pl.ds(pl.multiple_of(me * chans, chans), chans)

    def lane_slice(block):
        return pl.ds(pl.multiple_of(block * LANES, LANES), LANES)

    def head_slice(block):
        return pl.ds(pl.multiple_of(me * chans + block * LANES, LANES), LANES)

    def wide_slice(block):
        return pl.ds(pl.multiple_of(block * micro * LANES, LANES), micro * LANES)

    def loop(low, high, step_of):
        def run(index, carry):
            step_of(index)
            return carry

        lax.fori_loop(low, high, run, 0)

    def swap(axis, count, mine, out_ref, in_ref, sems):
        def copy(step):
            return pltpu.make_async_remote_copy(
                src_ref=out_ref,
                dst_ref=in_ref.at[mine],
                send_sem=sems.at[0, step],
                recv_sem=sems.at[1, step],
                device_id={axis: lax.rem(mine + step, count)},
                device_id_type=MESH,
            )

        loop(1, count, lambda step: copy(step).start())
        in_ref[mine] = out_ref[...]
        return lambda: loop(1, count, lambda step: copy(step).wait())

    def start_stats(slot, first, second):
        stat_out[slot, 0] = first
        stat_out[slot, 1] = second
        wait = swap(
            "section", sections, me, stat_out.at[slot], stat_in.at[slot], stat_sems.at[slot]
        )

        def finish():
            wait()
            return jnp.sum(stat_in[slot], axis=0)

        return finish

    def weight_copies(step):
        peer = lax.rem(me + step, sections)
        lanes = pl.ds(pl.multiple_of(peer * chans, chans), chans)
        rows = pl.ds(pl.multiple_of(peer * group_rows, group_rows), group_rows)
        return [
            pltpu.make_async_remote_copy(
                src_ref=source,
                dst_ref=target,
                send_sem=weight_sems.at[0, kind, step],
                recv_sem=weight_sems.at[1, kind, step],
                device_id={"section": peer},
                device_id_type=MESH,
            )
            for kind, source, target in (
                (0, gain_hbm.at[:, lanes], gain_ref.at[me]),
                (2, short_hbm.at[:, :, lanes], short_ref.at[me]),
                (1, taps_hbm.at[rows, :], taps_ref.at[me]),
            )
        ]

    def start_weights(step):
        for copy in weight_copies(step):
            copy.start()

    def wait_weights(step):
        for copy in weight_copies(step):
            copy.wait()

    own_rows = pl.ds(pl.multiple_of(me * group_rows, group_rows), group_rows)
    local_copies = [
        pltpu.make_async_copy(comp_ref.at[:, own_lanes], rows_in.at[0], local_sem.at[0]),
        pltpu.make_async_copy(gain_hbm.at[:, own_lanes], gain_ref.at[me], local_sem.at[1]),
        pltpu.make_async_copy(short_hbm.at[:, :, own_lanes], short_ref.at[me], local_sem.at[3]),
        pltpu.make_async_copy(taps_hbm.at[own_rows, :], taps_ref.at[me], local_sem.at[2]),
    ]

    def spread_copy(step):
        peer = lax.rem(me + step, sections)
        lanes = pl.ds(pl.multiple_of(peer * chans, chans), chans)
        return pltpu.make_async_remote_copy(
            src_ref=prompt_ref.at[:, lanes],
            dst_ref=pool.at[me, me_resp],
            send_sem=spread_sems.at[0, step],
            recv_sem=spread_sems.at[1, step],
            device_id={"section": peer},
            device_id_type=MESH,
        )

    def pool_copy(s, step):
        return pltpu.make_async_remote_copy(
            src_ref=pool.at[s, me_resp],
            dst_ref=pool.at[s, me_resp],
            send_sem=pool_sems.at[0, s, step],
            recv_sem=pool_sems.at[1, s, step],
            device_id={"resp": lax.rem(me_resp + step, n_resp)},
            device_id_type=MESH,
        )

    def own_pool():
        return pltpu.make_async_copy(
            prompt_ref.at[:, own_lanes], pool.at[me, me_resp], local_sem.at[4]
        )

    def start_pool(s):
        step = lax.rem(me - s + sections, sections)

        @pl.when(step == 0)
        def _():
            own_pool().wait()

        @pl.when(step > 0)
        def _():
            spread_copy(step).wait()

        loop(1, n_resp, lambda d: pool_copy(s, d).start())

    def wait_pool(s):
        loop(1, n_resp, lambda d: pool_copy(s, d).wait())

    loop(1, sections, start_weights)
    if direct:
        own_pool().start()
        loop(1, sections, lambda step: spread_copy(step).start())
    for copy in local_copies:
        copy.start()
    if direct:
        start_pool(0)
    for copy in local_copies:
        copy.wait()

    def first_stats(block):
        wide = rows_in[0, :, lane_slice(block)].astype(F32)
        stat_acc[...] += wide * wide

    stat_acc[...] = jnp.zeros_like(stat_acc)
    loop(0, blocks, first_stats)
    loop(1, sections, wait_weights)

    t_row = lax.broadcasted_iota(jnp.int32, (length, LANES), 0)
    s_lane = lax.broadcasted_iota(jnp.int32, (length, LANES), 1)
    keep = s_lane <= prompt_len + t_row
    s_row = lax.broadcasted_iota(jnp.int32, (total, LANES), 0)
    t_lane = lax.broadcasted_iota(jnp.int32, (total, LANES), 1)
    keep_t = s_row <= prompt_len + t_lane

    def build(step):
        s, block = step // blocks, step % blocks
        rows = pl.ds(pl.multiple_of(block * groups, groups), groups)
        flipped = taps_ref[s, rows, :][:, :LANES]
        for g in range(groups):
            base = pl.multiple_of((block * groups + g) * length, length)
            wide = jnp.broadcast_to(flipped[g : g + 1], (length, LANES))
            wide = pltpu.roll(wide, prompt_len, 1, stride=1, stride_axis=0)
            wide = jnp.where(keep, wide, 0.0)
            high = wide.astype(BF16)
            low = (wide - high.astype(F32)).astype(BF16)
            toep[s, pl.ds(base, length), :] = jnp.concatenate([high, high, low], axis=1)

    def build_t(s, block):
        rows = pl.ds(pl.multiple_of(block * groups, groups), groups)
        plain = taps_ref[s, rows, :][:, LANES:]
        for g in range(groups):
            base = pl.multiple_of((block * groups + g) * total, total)
            wide = jnp.broadcast_to(plain[g : g + 1], (total, LANES))
            wide = pltpu.roll(wide, prompt_len, 1, stride=1, stride_axis=0)
            toep_t[s, pl.ds(base, total), :] = jnp.where(keep_t, wide, 0.0).astype(BF16)

    loop(0, sections * blocks, build)

    def choose(s, block):
        lanes = lane_slice(block)
        for m in range(micro):
            rows = slice(m * prompt_len, (m + 1) * prompt_len)
            if direct:
                picked = jnp.zeros((prompt_len, LANES), F32)
                for r in range(n_resp):
                    flag = jnp.full((prompt_len, LANES), owner_ref[m], jnp.int32) == r
                    picked = jnp.where(flag, pool[s, r, :, lanes].astype(F32), picked)
                chosen_rows[s, rows, lanes] = picked.astype(BF16)
            else:
                picked = prompt_ref[s, rows, lanes].astype(F32)
                chosen_rows[s, rows, lanes] = prompt_ref[s, rows, lanes]
            prompt_acc[rows, :] += picked * picked

    row_id = lax.broadcasted_iota(jnp.int32, (total, LANES), 0)
    wide_group = (
        lax.broadcasted_iota(jnp.int32, (1, micro * LANES), 1) % LANES
    ) // per_group
    tap_count = short_hbm.shape[0]

    def pick(stacked, rows):
        out = stacked[0:rows]
        for g in range(1, groups):
            out = jnp.where(wide_group == g, stacked[g * rows : (g + 1) * rows], out)
        return out

    def joined_rows(s, m, lanes):
        rows_p = slice(m * prompt_len, (m + 1) * prompt_len)
        rows_c = slice(m * length, (m + 1) * length)
        joined = jnp.concatenate(
            [chosen_rows[s, rows_p, lanes].astype(F32), rows_in[s, rows_c, lanes].astype(F32)],
            axis=0,
        )
        factor = jnp.concatenate([fac_p[s, rows_p, :], fac_c[s, rows_c, :]], axis=0)
        return joined, factor

    def forward(s, carry):
        if direct:
            wait_pool(s)

            @pl.when(s + 1 < sections)
            def _():
                start_pool(s + 1)

        prompt_acc[...] = jnp.zeros_like(prompt_acc)
        loop(0, blocks, lambda block: choose(s, block))
        finish = start_stats(s, rows_to_line(stat_acc[...]), rows_to_line(prompt_acc[...]))
        loop(0, blocks, lambda block: build_t(s, block))
        sums = finish()
        fac_c[s] = lax.rsqrt(line_to_rows(sums[0]) * (1.0 / width) + 1e-06)
        fac_p[s] = lax.rsqrt(line_to_rows(sums[1]) * (1.0 / width) + 1e-06)
        stat_acc[...] = jnp.zeros_like(stat_acc)
        score_acc[...] = jnp.zeros_like(score_acc)

        def run(block, carry):
            lanes = lane_slice(block)
            wide = wide_slice(block)
            gain = gain_ref[s, :, lanes]
            short = jnp.concatenate(
                [short_ref[s, j, :, lanes] for j in range(tap_count)], axis=0
            )
            parts, lows, saved = [], [], []
            for m in range(micro):
                joined, factor = joined_rows(s, m, lanes)
                normed = joined * factor * gain
                shorter = normed * short[0:1]
                for j in range(1, tap_count):
                    moved = jnp.where(row_id >= j, pltpu.roll(normed, j, 0), 0.0)
                    shorter = shorter + moved * short[j : j + 1]
                high = shorter.astype(BF16)
                parts.append(high)
                lows.append((shorter - high.astype(F32)).astype(BF16))
                saved.append((joined[prompt_len:], normed[prompt_len:]))
            high = jnp.concatenate(parts, axis=1)
            short_out[s, :, wide] = high
            rhs = jnp.concatenate([high, jnp.concatenate(lows, axis=1), high], axis=0)
            base = pl.multiple_of(block * groups * length, groups * length)
            stacked = jnp.dot(
                toep[s, pl.ds(base, groups * length), :], rhs, preferred_element_type=F32
            )
            longer_all = pick(stacked, length)
            for m in range(micro):
                rows = slice(m * length, (m + 1) * length)
                longer = longer_all[:, m * LANES : (m + 1) * LANES]
                long_out[s, rows, lanes] = longer
                mixed = (saved[m][0] + saved[m][1] * longer).astype(BF16)
                rows_in[s + 1, rows, lanes] = mixed
                mixed = mixed.astype(F32)
                stat_acc[rows, :] += mixed * mixed
                score_acc[rows, :] += mixed * head_ref[0:1, head_slice(block)]
            return carry

        lax.fori_loop(0, blocks, run, 0)

        return carry

    lax.fori_loop(0, sections, forward, 0)

    live = []
    for m in range(micro):
        count = jnp.full((length, LANES), length_ref[m, 0], jnp.int32)
        live.append(jnp.where(t_row < count, 1.0, 0.0) / jnp.sqrt(count.astype(F32)))
    tile_rows = []
    for m in range(micro):
        rows = slice(m * length, (m + 1) * length)
        line = jnp.sum(score_acc[rows, :] * live[m], axis=0, keepdims=True)
        tile_rows.append(jnp.broadcast_to(jnp.sum(line, axis=1, keepdims=True), (1, LANES)))
    tile_rows.append(jnp.zeros((8 - micro, LANES), F32))
    score_tile = jnp.concatenate(tile_rows, axis=0)
    own_score = start_stats(sections, score_tile, score_tile)()[0]
    score_ref[...] = own_score
    resp_out[...] = own_score
    swap("resp", n_resp, me_resp, resp_out, resp_in, resp_sems)()
    winner, loser = ends_ref[0], ends_ref[1]

    def signs(r):
        return jnp.where(winner == r, 1.0, 0.0) - jnp.where(loser == r, 1.0, 0.0)

    margin = lax.fori_loop(
        0, n_resp, lambda r, acc: acc + resp_in[r] * signs(r), jnp.zeros((8, LANES), F32)
    )
    weight = 1.0 / (1.0 + jnp.exp(margin))
    slopes = -jnp.sum(signs(me_resp) * weight, axis=1, keepdims=True)

    def seed(block, carry):
        lanes = lane_slice(block)
        for m in range(micro):
            rows = slice(m * length, (m + 1) * length)
            upstream[rows, lanes] = live[m] * slopes[m : m + 1] * head_ref[0:1, head_slice(block)]
        return carry

    lax.fori_loop(0, blocks, seed, 0)

    keep_pair = total - 1 - s_lane <= prompt_len + t_row
    reverse = (
        lax.broadcasted_iota(jnp.int32, (total, total), 0)
        + lax.broadcasted_iota(jnp.int32, (total, total), 1)
        == total - 1
    )
    reverse = jnp.where(reverse, 1.0, 0.0).astype(BF16)

    share = 2 * blocks // n_resp

    def part_slice(r):
        return pl.ds(r * share, share)

    def part_steps(s, action):
        def each(step):
            peer = lax.rem(me_resp + step, n_resp)
            action(
                pltpu.make_async_remote_copy(
                    src_ref=tiles_own.at[s, part_slice(peer)],
                    dst_ref=tiles_in.at[s, me_resp],
                    send_sem=part_sems.at[0, s, step],
                    recv_sem=part_sems.at[1, s, step],
                    device_id={"resp": peer},
                    device_id_type=MESH,
                )
            )

        loop(1, n_resp, each)

    def tile_copy(s, step, k, r):
        return pltpu.make_async_remote_copy(
            src_ref=tiles_sum.at[s],
            dst_ref=tiles_all.at[k, r],
            send_sem=tile_send.at[s, step],
            recv_sem=tile_recv.at[k, r],
            device_id={"section": s, "resp": lax.rem(me_resp + step, n_resp)},
            device_id_type=MESH,
        )

    def tile_steps(s, action):
        def each(step):
            @pl.when(jnp.logical_not((s == me) & (step == 0)))
            def _():
                action(tile_copy(s, step, me, me_resp))

        loop(0, n_resp, each)

    def backward(step, carry):
        s = sections - 1 - step
        stat_acc[...] = jnp.zeros_like(stat_acc)

        def run(block, carry):
            lanes = lane_slice(block)
            wide = wide_slice(block)
            gain = gain_ref[s, :, lanes]
            short = jnp.concatenate(
                [short_ref[s, j, :, lanes] for j in range(tap_count)], axis=0
            )
            parts, saved = [], []
            for m in range(micro):
                rows = slice(m * length, (m + 1) * length)
                joined, factor = joined_rows(s, m, lanes)
                scaled = joined * factor
                normed = scaled * gain
                above = upstream[rows, lanes]
                parts.append((above * normed[prompt_len:]).astype(BF16))
                saved.append((joined[prompt_len:], scaled, normed, above))
            d_long = jnp.concatenate(parts, axis=1)
            base = pl.multiple_of(block * groups * total, groups * total)
            stacked = jnp.dot(
                toep_t[s, pl.ds(base, groups * total), :][:, :length],
                d_long,
                preferred_element_type=F32,
            )
            d_short_all = pick(stacked, total)
            turned = jnp.dot(reverse, short_out[s, :, wide], preferred_element_type=F32)
            d_wide = d_long.astype(F32)
            masked = jnp.concatenate(
                [
                    jnp.where(wide_group == g, d_wide, 0.0).astype(BF16)
                    for g in range(groups)
                ],
                axis=0,
            )
            pairs = lax.dot_general(
                masked,
                turned.astype(BF16),
                (((1,), (1,)), ((), ())),
                preferred_element_type=F32,
            )
            lines = []
            for g in range(groups):
                one = jnp.where(keep_pair, pairs[g * length : (g + 1) * length], 0.0)
                one = pltpu.roll(one, LANES + 1 - length, 1, stride=1, stride_axis=0)
                lines.append(jnp.sum(one, axis=0, keepdims=True))
            tiles_own[s, 2 * block + 1] = jnp.concatenate(lines, axis=0)
            grads = [jnp.zeros((1, LANES), F32)] * (tap_count + 1)
            for m in range(micro):
                rows = slice(m * length, (m + 1) * length)
                joined_c, scaled, normed, above = saved[m]
                d_short = d_short_all[:, m * LANES : (m + 1) * LANES]
                d_normed = d_short * short[0:1]
                grads[1] = grads[1] + jnp.sum(d_short * normed, axis=0, keepdims=True)
                for j in range(1, tap_count):
                    moved = jnp.where(
                        row_id < total - j, pltpu.roll(d_short, total - j, 0), 0.0
                    )
                    d_normed = d_normed + moved * short[j : j + 1]
                    grads[1 + j] = grads[1 + j] + jnp.sum(
                        moved * normed, axis=0, keepdims=True
                    )
                direct = above * long_out[s, rows, lanes]
                d_normed = jnp.concatenate(
                    [d_normed[:prompt_len], d_normed[prompt_len:] + direct], axis=0
                )
                grads[0] = grads[0] + jnp.sum(d_normed * scaled, axis=0, keepdims=True)
                inner = d_normed[prompt_len:] * gain
                partial[rows, lanes] = inner
                stat_acc[rows, :] += inner * joined_c
            tiles_own[s, 2 * block] = jnp.concatenate(grads, axis=0)
            return carry

        lax.fori_loop(0, blocks, run, 0)

        if direct:
            part_steps(s, lambda copy: copy.start())
            parts_in = tiles_in.at[s]
            parts_in[me_resp] = tiles_own[s, part_slice(me_resp)]

        @pl.when(s > 0)
        def _():
            line = rows_to_line(stat_acc[...])
            all_sums = start_stats(sections + 1 + step, line, line)()[0]
            factor = fac_c[s]
            pull = line_to_rows(all_sums) * (1.0 / width) * factor * factor * factor

            def finish(block, carry):
                lanes = lane_slice(block)
                grad = (
                    upstream[:, lanes]
                    + factor * partial[:, lanes]
                    - rows_in[s, :, lanes].astype(F32) * pull
                )
                upstream[:, lanes] = grad.astype(BF16).astype(F32)
                return carry

            lax.fori_loop(0, blocks, finish, 0)

        if direct:
            part_steps(s, lambda copy: copy.wait())
            tiles_sum[s] = jnp.sum(tiles_in[s], axis=0)

            @pl.when(s == me)
            def _():
                tiles_all[me, me_resp] = tiles_sum[s]

            tile_steps(s, lambda copy: copy.start())

        return carry

    lax.fori_loop(0, sections, backward, 0)

    if direct:
        loop(0, sections, lambda s: tile_steps(s, lambda copy: copy.wait_send()))

        def arrive(step):
            k, r = step // n_resp, step % n_resp

            @pl.when(jnp.logical_not((k == me) & (r == me_resp)))
            def _():
                tile_copy(0, 0, k, r).wait_recv()

        loop(0, sections * n_resp, arrive)
        gain_out, taps_short_out, taps_long_out = outs
        per_line = LANES // groups
        for line in range(sections * blocks // per_line):
            lines = []
            for place in range(per_line):
                block = line * per_line + place
                lanes = slice(block * LANES, (block + 1) * LANES)
                owner, local = divmod(2 * block, 2 * blocks)
                first, second = (divmod(local + kind, share) for kind in range(2))
                tile = tiles_all[owner, first[0], first[1]]
                gain_out[:, lanes] = tile[0:1]
                for j in range(tap_count):
                    taps_short_out[j, :, lanes] = tile[1 + j : 2 + j]
                lines.append(tiles_all[owner, second[0], second[1]])
            lanes = slice(line * LANES, (line + 1) * LANES)
            taps_long_out[0, :, lanes] = jnp.transpose(jnp.concatenate(lines, axis=0))
    else:
        outs[0][...] = tiles_own[...]


def run_kernel(dims, direct, *arrays):
    sections, n_resp, micro, length, prompt_len, chans, per_group, width = dims
    rows = micro * length
    total = prompt_len + length
    group_total = chans // per_group
    tile = (8, LANES)
    tiles = 2 * chans // LANES
    share = tiles // n_resp if direct else 1
    ranks = n_resp if direct else 1
    vmem = pl.BlockSpec(memory_space=pltpu.VMEM)
    hbm = pl.BlockSpec(memory_space=pl.ANY)
    smem = pl.BlockSpec(memory_space=pltpu.SMEM)
    tap_count = arrays[3].shape[0]
    if direct:
        out_shapes = [(1, width), (tap_count, 1, width), (1, LANES, width // per_group)]
    else:
        out_shapes = [(sections, tiles) + tile]
    return pl.pallas_call(
        functools.partial(kernel, dims, direct),
        out_shape=(
            jax.ShapeDtypeStruct(tile, F32),
            *(jax.ShapeDtypeStruct(shape, F32) for shape in out_shapes),
        ),
        in_specs=[hbm, hbm if direct else vmem, hbm, hbm, hbm, smem, vmem, vmem, smem],
        out_specs=(vmem,) * (1 + len(out_shapes)),
        scratch_shapes=[
            pltpu.VMEM((sections, group_total * length, 3 * LANES), BF16),
            pltpu.VMEM((sections, group_total * total, LANES), BF16),
            pltpu.VMEM((sections, ranks, prompt_len, chans), BF16),
            pltpu.VMEM((sections, micro * prompt_len, chans), BF16),
            pltpu.VMEM((sections, 1, chans), F32),
            pltpu.VMEM((sections, tap_count, 1, chans), F32),
            pltpu.VMEM((sections, group_total, 2 * LANES), F32),
            pltpu.VMEM((sections + 1, rows, chans), BF16),
            pltpu.VMEM((sections, total, micro * chans), BF16),
            pltpu.VMEM((sections, rows, chans), F32),
            pltpu.VMEM((sections, micro * prompt_len, LANES), F32),
            pltpu.VMEM((sections, rows, LANES), F32),
            pltpu.VMEM((rows, chans), F32),
            pltpu.VMEM((rows, chans), F32),
            pltpu.VMEM((rows, LANES), F32),
            pltpu.VMEM((rows, LANES), F32),
            pltpu.VMEM((micro * prompt_len, LANES), F32),
            pltpu.VMEM((2 * sections, 2) + tile, F32),
            pltpu.VMEM((2 * sections, sections, 2) + tile, F32),
            pltpu.VMEM(tile, F32),
            pltpu.VMEM((n_resp,) + tile, F32),
            pltpu.VMEM((sections, tiles) + tile, F32),
            pltpu.VMEM((sections, ranks, share) + tile, F32),
            pltpu.VMEM((sections, share) + tile, F32),
            pltpu.VMEM((sections, ranks, share) + tile, F32),
            pltpu.SemaphoreType.DMA((5,)),
            pltpu.SemaphoreType.DMA((2, 3, sections)),
            pltpu.SemaphoreType.DMA((2, sections)),
            pltpu.SemaphoreType.DMA((2, sections, ranks)),
            pltpu.SemaphoreType.DMA((2 * sections, 2, sections)),
            pltpu.SemaphoreType.DMA((2, n_resp)),
            pltpu.SemaphoreType.DMA((2, sections, ranks)),
            pltpu.SemaphoreType.DMA((sections, ranks)),
            pltpu.SemaphoreType.DMA((sections, ranks)),
        ],
        compiler_params=pltpu.CompilerParams(
            has_side_effects=True, vmem_limit_bytes=56 * 1024 * 1024
        ),
    )(*arrays)


def body(
    completion_rows,
    prompt_pool,
    norm_gain,
    short_taps,
    long_taps,
    score_head,
    live_lengths,
    prompt_owner,
    pair_index,
):
    sections = lax.axis_size("section")
    n_resp = lax.axis_size("resp")
    me_resp = lax.axis_index("resp")
    micro, _, length, width = completion_rows.shape
    prompt_len = prompt_pool.shape[2]
    chans = width // sections
    tap_len, group_all = long_taps.shape[1:]
    per_group = width // group_all
    dims = (sections, n_resp, micro, length, prompt_len, chans, per_group, width)

    tiles = 2 * chans // LANES
    direct = n_resp <= 8 and tiles % n_resp == 0

    taps = long_taps[0].T
    flipped = jnp.concatenate([taps[:, :1], taps[:, :0:-1]], axis=1)
    taps = jnp.concatenate([flipped, taps], axis=1)
    prompts = prompt_pool[0, 0]
    if not direct:
        split = prompts.reshape(prompt_len, sections, chans).transpose(1, 0, 2)
        split = lax.all_to_all(split, "section", 0, 0, tiled=True)
        here = (prompt_owner == me_resp)[None, :, None, None]
        split = lax.psum(jnp.where(here, split[:, None], jnp.zeros((), BF16)), "resp")
        prompts = split.reshape(sections, micro * prompt_len, chans)
    rows = completion_rows.reshape(micro * length, width)
    head = score_head[None]

    ends = jnp.pad(
        pair_index.transpose(2, 0, 1),
        ((0, 0), (0, 8 - micro), (0, LANES - pair_index.shape[1])),
        constant_values=-1,
    )
    scores, *grads = run_kernel(
        dims,
        direct,
        rows,
        prompts,
        norm_gain,
        short_taps.transpose(1, 0, 2),
        taps,
        prompt_owner,
        head,
        ends,
        live_lengths,
    )
    scores = scores[:micro, :1].astype(BF16)
    if direct:
        return (scores, grads[0], grads[1].transpose(1, 0, 2), grads[2])
    grads = lax.psum(grads[0], "resp")
    grads = lax.all_to_all(grads, "section", 0, 0, tiled=True)
    grads = grads.reshape(sections * tiles // 2, 2, 8, LANES)
    gs_grad = grads[:, 0].transpose(1, 0, 2).reshape(8, width)
    taps_grad = grads[:, 1].reshape(group_all, tap_len).T
    return (
        scores,
        gs_grad[:1],
        gs_grad[None, 1:],
        taps_grad[None],
    )


def solution(mesh):
    placed = (
        P(None, ("groups", "resp"), None, None),
        P("section", ("groups", "resp"), None, None),
        P("section", None),
        P("section", None, None),
        P("section", None, None),
        P(),
        P(None, ("groups", "resp")),
        P("groups"),
        P(None, "groups", None),
    )
    return jax.shard_map(
        body,
        mesh=mesh,
        in_specs=placed,
        out_specs=(
            P(None, ("groups", "resp")),
            P("section", "groups"),
            P("section", "groups", None),
            P("section", "groups", None),
        ),
        check_vma=False,
    )
```

```python
import functools

import jax
import jax.numpy as jnp
from jax import lax
from jax.experimental import pallas as pl
from jax.experimental.pallas import tpu as pltpu
from jax.sharding import PartitionSpec as P

LANES = 128
MESH = pl.DeviceIdType.MESH
F32 = jnp.float32
BF16 = jnp.bfloat16


def rows_to_line(block):
    line = jnp.sum(jnp.transpose(block), axis=0, keepdims=True)
    return jnp.broadcast_to(line, (8, LANES))


def line_to_rows(tile):
    return jnp.transpose(jnp.broadcast_to(tile[0:1], (LANES, LANES)))


def kernel(
    dims,
    direct,
    comp_ref,
    prompt_ref,
    gain_hbm,
    short_hbm,
    taps_hbm,
    owner_ref,
    head_ref,
    ends_ref,
    length_ref,
    score_ref,
    *rest,
):
    sections, n_resp, micro, length, prompt_len, chans, per_group, width = dims
    outs, rest = (rest[:3], rest[3:]) if direct else (rest[:1], rest[1:])
    (
        toep,
        toep_t,
        pool,
        chosen_rows,
        gain_ref,
        short_ref,
        taps_ref,
        rows_in,
        short_out,
        long_out,
        fac_p,
        fac_c,
        upstream,
        partial,
        stat_acc,
        score_acc,
        prompt_acc,
        stat_out,
        stat_in,
        resp_out,
        resp_in,
        tiles_own,
        tiles_in,
        tiles_sum,
        tiles_all,
        local_sem,
        weight_sems,
        spread_sems,
        pool_sems,
        stat_sems,
        resp_sems,
        part_sems,
        tile_send,
        tile_recv,
    ) = rest
    groups = LANES // per_group
    blocks = chans // LANES
    group_rows = blocks * groups
    total = prompt_len + length
    me = lax.axis_index("section")
    me_resp = lax.axis_index("resp")
    own_lanes = pl.ds(pl.multiple_of(me * chans, chans), chans)

    def lane_slice(block):
        return pl.ds(pl.multiple_of(block * LANES, LANES), LANES)

    def head_slice(block):
        return pl.ds(pl.multiple_of(me * chans + block * LANES, LANES), LANES)

    def wide_slice(block):
        return pl.ds(pl.multiple_of(block * micro * LANES, LANES), micro * LANES)

    def loop(low, high, step_of):
        def run(index, carry):
            step_of(index)
            return carry

        lax.fori_loop(low, high, run, 0)

    def swap(axis, count, mine, out_ref, in_ref, sems):
        def copy(step):
            return pltpu.make_async_remote_copy(
                src_ref=out_ref,
                dst_ref=in_ref.at[mine],
                send_sem=sems.at[0, step],
                recv_sem=sems.at[1, step],
                device_id={axis: lax.rem(mine + step, count)},
                device_id_type=MESH,
            )

        loop(1, count, lambda step: copy(step).start())
        in_ref[mine] = out_ref[...]
        return lambda: loop(1, count, lambda step: copy(step).wait())

    def start_stats(slot, first, second):
        stat_out[slot, 0] = first
        stat_out[slot, 1] = second
        wait = swap(
            "section", sections, me, stat_out.at[slot], stat_in.at[slot], stat_sems.at[slot]
        )

        def finish():
            wait()
            return jnp.sum(stat_in[slot], axis=0)

        return finish

    def weight_copies(step):
        peer = lax.rem(me + step, sections)
        lanes = pl.ds(pl.multiple_of(peer * chans, chans), chans)
        rows = pl.ds(pl.multiple_of(peer * group_rows, group_rows), group_rows)
        return [
            pltpu.make_async_remote_copy(
                src_ref=source,
                dst_ref=target,
                send_sem=weight_sems.at[0, kind, step],
                recv_sem=weight_sems.at[1, kind, step],
                device_id={"section": peer},
                device_id_type=MESH,
            )
            for kind, source, target in (
                (0, gain_hbm.at[:, lanes], gain_ref.at[me]),
                (2, short_hbm.at[:, :, lanes], short_ref.at[me]),
                (1, taps_hbm.at[rows, :], taps_ref.at[me]),
            )
        ]

    def start_weights(step):
        for copy in weight_copies(step):
            copy.start()

    def wait_weights(step):
        for copy in weight_copies(step):
            copy.wait()

    own_rows = pl.ds(pl.multiple_of(me * group_rows, group_rows), group_rows)
    local_copies = [
        pltpu.make_async_copy(comp_ref.at[:, own_lanes], rows_in.at[0], local_sem.at[0]),
        pltpu.make_async_copy(gain_hbm.at[:, own_lanes], gain_ref.at[me], local_sem.at[1]),
        pltpu.make_async_copy(short_hbm.at[:, :, own_lanes], short_ref.at[me], local_sem.at[3]),
        pltpu.make_async_copy(taps_hbm.at[own_rows, :], taps_ref.at[me], local_sem.at[2]),
    ]

    def spread_copy(step):
        peer = lax.rem(me + step, sections)
        lanes = pl.ds(pl.multiple_of(peer * chans, chans), chans)
        return pltpu.make_async_remote_copy(
            src_ref=prompt_ref.at[:, lanes],
            dst_ref=pool.at[me, me_resp],
            send_sem=spread_sems.at[0, step],
            recv_sem=spread_sems.at[1, step],
            device_id={"section": peer},
            device_id_type=MESH,
        )

    def pool_copy(s, step):
        return pltpu.make_async_remote_copy(
            src_ref=pool.at[s, me_resp],
            dst_ref=pool.at[s, me_resp],
            send_sem=pool_sems.at[0, s, step],
            recv_sem=pool_sems.at[1, s, step],
            device_id={"resp": lax.rem(me_resp + step, n_resp)},
            device_id_type=MESH,
        )

    def own_pool():
        return pltpu.make_async_copy(
            prompt_ref.at[:, own_lanes], pool.at[me, me_resp], local_sem.at[4]
        )

    def start_pool(s):
        step = lax.rem(me - s + sections, sections)

        @pl.when(step == 0)
        def _():
            own_pool().wait()

        @pl.when(step > 0)
        def _():
            spread_copy(step).wait()

        loop(1, n_resp, lambda d: pool_copy(s, d).start())

    def wait_pool(s):
        loop(1, n_resp, lambda d: pool_copy(s, d).wait())

    loop(1, sections, start_weights)
    if direct:
        own_pool().start()
        loop(1, sections, lambda step: spread_copy(step).start())
    for copy in local_copies:
        copy.start()
    if direct:
        for s in range(min(2, sections)):
            start_pool(s)
    for copy in local_copies:
        copy.wait()

    def first_stats(block):
        wide = rows_in[0, :, lane_slice(block)].astype(F32)
        stat_acc[...] += wide * wide

    stat_acc[...] = jnp.zeros_like(stat_acc)
    loop(0, blocks, first_stats)
    loop(1, sections, wait_weights)

    t_row = lax.broadcasted_iota(jnp.int32, (length, LANES), 0)
    s_lane = lax.broadcasted_iota(jnp.int32, (length, LANES), 1)
    keep = s_lane <= prompt_len + t_row
    s_row = lax.broadcasted_iota(jnp.int32, (total, LANES), 0)
    t_lane = lax.broadcasted_iota(jnp.int32, (total, LANES), 1)
    keep_t = s_row <= prompt_len + t_lane

    def build(step):
        s, block = step // blocks, step % blocks
        rows = pl.ds(pl.multiple_of(block * groups, groups), groups)
        flipped = taps_ref[s, rows, :][:, :LANES]
        for g in range(groups):
            base = pl.multiple_of((block * groups + g) * length, length)
            wide = jnp.broadcast_to(flipped[g : g + 1], (length, LANES))
            wide = pltpu.roll(wide, prompt_len, 1, stride=1, stride_axis=0)
            wide = jnp.where(keep, wide, 0.0)
            high = wide.astype(BF16)
            low = (wide - high.astype(F32)).astype(BF16)
            toep[s, pl.ds(base, length), :] = jnp.concatenate([high, high, low], axis=1)

    def build_t(s, block):
        rows = pl.ds(pl.multiple_of(block * groups, groups), groups)
        plain = taps_ref[s, rows, :][:, LANES:]
        for g in range(groups):
            base = pl.multiple_of((block * groups + g) * total, total)
            wide = jnp.broadcast_to(plain[g : g + 1], (total, LANES))
            wide = pltpu.roll(wide, prompt_len, 1, stride=1, stride_axis=0)
            toep_t[s, pl.ds(base, total), :] = jnp.where(keep_t, wide, 0.0).astype(BF16)

    loop(0, sections * blocks, build)

    def choose(s, block):
        lanes = lane_slice(block)
        for m in range(micro):
            rows = slice(m * prompt_len, (m + 1) * prompt_len)
            if direct:
                picked = jnp.zeros((prompt_len, LANES), F32)
                for r in range(n_resp):
                    flag = jnp.full((prompt_len, LANES), owner_ref[m], jnp.int32) == r
                    picked = jnp.where(flag, pool[s, r, :, lanes].astype(F32), picked)
                chosen_rows[s, rows, lanes] = picked.astype(BF16)
            else:
                picked = prompt_ref[s, rows, lanes].astype(F32)
                chosen_rows[s, rows, lanes] = prompt_ref[s, rows, lanes]
            prompt_acc[rows, :] += picked * picked

    row_id = lax.broadcasted_iota(jnp.int32, (total, LANES), 0)
    wide_group = (
        lax.broadcasted_iota(jnp.int32, (1, micro * LANES), 1) % LANES
    ) // per_group
    tap_count = short_hbm.shape[0]

    def pick(stacked, rows):
        out = stacked[0:rows]
        for g in range(1, groups):
            out = jnp.where(wide_group == g, stacked[g * rows : (g + 1) * rows], out)
        return out

    def joined_rows(s, m, lanes):
        rows_p = slice(m * prompt_len, (m + 1) * prompt_len)
        rows_c = slice(m * length, (m + 1) * length)
        joined = jnp.concatenate(
            [chosen_rows[s, rows_p, lanes].astype(F32), rows_in[s, rows_c, lanes].astype(F32)],
            axis=0,
        )
        factor = jnp.concatenate([fac_p[s, rows_p, :], fac_c[s, rows_c, :]], axis=0)
        return joined, factor

    def forward(s, carry):
        if direct:
            wait_pool(s)

            @pl.when(s + 2 < sections)
            def _():
                start_pool(s + 2)

        prompt_acc[...] = jnp.zeros_like(prompt_acc)
        loop(0, blocks, lambda block: choose(s, block))
        finish = start_stats(s, rows_to_line(stat_acc[...]), rows_to_line(prompt_acc[...]))
        loop(0, blocks, lambda block: build_t(s, block))
        sums = finish()
        fac_c[s] = lax.rsqrt(line_to_rows(sums[0]) * (1.0 / width) + 1e-06)
        fac_p[s] = lax.rsqrt(line_to_rows(sums[1]) * (1.0 / width) + 1e-06)
        stat_acc[...] = jnp.zeros_like(stat_acc)
        score_acc[...] = jnp.zeros_like(score_acc)

        def run(block, carry):
            lanes = lane_slice(block)
            wide = wide_slice(block)
            gain = gain_ref[s, :, lanes]
            short = jnp.concatenate(
                [short_ref[s, j, :, lanes] for j in range(tap_count)], axis=0
            )
            parts, lows, saved = [], [], []
            for m in range(micro):
                joined, factor = joined_rows(s, m, lanes)
                normed = joined * factor * gain
                shorter = normed * short[0:1]
                for j in range(1, tap_count):
                    moved = jnp.where(row_id >= j, pltpu.roll(normed, j, 0), 0.0)
                    shorter = shorter + moved * short[j : j + 1]
                high = shorter.astype(BF16)
                parts.append(high)
                lows.append((shorter - high.astype(F32)).astype(BF16))
                saved.append((joined[prompt_len:], normed[prompt_len:]))
            high = jnp.concatenate(parts, axis=1)
            short_out[s, :, wide] = high
            rhs = jnp.concatenate([high, jnp.concatenate(lows, axis=1), high], axis=0)
            base = pl.multiple_of(block * groups * length, groups * length)
            stacked = jnp.dot(
                toep[s, pl.ds(base, groups * length), :], rhs, preferred_element_type=F32
            )
            longer_all = pick(stacked, length)
            for m in range(micro):
                rows = slice(m * length, (m + 1) * length)
                longer = longer_all[:, m * LANES : (m + 1) * LANES]
                long_out[s, rows, lanes] = longer
                mixed = (saved[m][0] + saved[m][1] * longer).astype(BF16)
                rows_in[s + 1, rows, lanes] = mixed
                mixed = mixed.astype(F32)
                stat_acc[rows, :] += mixed * mixed
                score_acc[rows, :] += mixed * head_ref[0:1, head_slice(block)]
            return carry

        lax.fori_loop(0, blocks, run, 0)

        return carry

    lax.fori_loop(0, sections, forward, 0)

    live = []
    for m in range(micro):
        count = jnp.full((length, LANES), length_ref[m, 0], jnp.int32)
        live.append(jnp.where(t_row < count, 1.0, 0.0) / jnp.sqrt(count.astype(F32)))
    tile_rows = []
    for m in range(micro):
        rows = slice(m * length, (m + 1) * length)
        line = jnp.sum(score_acc[rows, :] * live[m], axis=0, keepdims=True)
        tile_rows.append(jnp.broadcast_to(jnp.sum(line, axis=1, keepdims=True), (1, LANES)))
    tile_rows.append(jnp.zeros((8 - micro, LANES), F32))
    score_tile = jnp.concatenate(tile_rows, axis=0)
    own_score = start_stats(sections, score_tile, score_tile)()[0]
    score_ref[...] = own_score
    resp_out[...] = own_score
    swap("resp", n_resp, me_resp, resp_out, resp_in, resp_sems)()
    winner, loser = ends_ref[0], ends_ref[1]

    def signs(r):
        return jnp.where(winner == r, 1.0, 0.0) - jnp.where(loser == r, 1.0, 0.0)

    margin = lax.fori_loop(
        0, n_resp, lambda r, acc: acc + resp_in[r] * signs(r), jnp.zeros((8, LANES), F32)
    )
    weight = 1.0 / (1.0 + jnp.exp(margin))
    slopes = -jnp.sum(signs(me_resp) * weight, axis=1, keepdims=True)

    def seed(block, carry):
        lanes = lane_slice(block)
        for m in range(micro):
            rows = slice(m * length, (m + 1) * length)
            upstream[rows, lanes] = live[m] * slopes[m : m + 1] * head_ref[0:1, head_slice(block)]
        return carry

    lax.fori_loop(0, blocks, seed, 0)

    keep_pair = total - 1 - s_lane <= prompt_len + t_row
    reverse = (
        lax.broadcasted_iota(jnp.int32, (total, total), 0)
        + lax.broadcasted_iota(jnp.int32, (total, total), 1)
        == total - 1
    )
    reverse = jnp.where(reverse, 1.0, 0.0).astype(BF16)

    share = 2 * blocks // n_resp

    def part_slice(r):
        return pl.ds(r * share, share)

    def part_steps(s, action):
        def each(step):
            peer = lax.rem(me_resp + step, n_resp)
            action(
                pltpu.make_async_remote_copy(
                    src_ref=tiles_own.at[s, part_slice(peer)],
                    dst_ref=tiles_in.at[s, me_resp],
                    send_sem=part_sems.at[0, s, step],
                    recv_sem=part_sems.at[1, s, step],
                    device_id={"resp": peer},
                    device_id_type=MESH,
                )
            )

        loop(1, n_resp, each)

    def tile_copy(s, step, k, r):
        return pltpu.make_async_remote_copy(
            src_ref=tiles_sum.at[s],
            dst_ref=tiles_all.at[k, r],
            send_sem=tile_send.at[s, step],
            recv_sem=tile_recv.at[k, r],
            device_id={"section": s, "resp": lax.rem(me_resp + step, n_resp)},
            device_id_type=MESH,
        )

    def tile_steps(s, action):
        def each(step):
            @pl.when(jnp.logical_not((s == me) & (step == 0)))
            def _():
                action(tile_copy(s, step, me, me_resp))

        loop(0, n_resp, each)

    def backward(step, carry):
        s = sections - 1 - step
        stat_acc[...] = jnp.zeros_like(stat_acc)

        def run(block, carry):
            lanes = lane_slice(block)
            wide = wide_slice(block)
            gain = gain_ref[s, :, lanes]
            short = jnp.concatenate(
                [short_ref[s, j, :, lanes] for j in range(tap_count)], axis=0
            )
            parts, saved = [], []
            for m in range(micro):
                rows = slice(m * length, (m + 1) * length)
                joined, factor = joined_rows(s, m, lanes)
                scaled = joined * factor
                normed = scaled * gain
                above = upstream[rows, lanes]
                parts.append((above * normed[prompt_len:]).astype(BF16))
                saved.append((joined[prompt_len:], scaled, normed, above))
            d_long = jnp.concatenate(parts, axis=1)
            base = pl.multiple_of(block * groups * total, groups * total)
            stacked = jnp.dot(
                toep_t[s, pl.ds(base, groups * total), :][:, :length],
                d_long,
                preferred_element_type=F32,
            )
            d_short_all = pick(stacked, total)
            turned = jnp.dot(reverse, short_out[s, :, wide], preferred_element_type=F32)
            d_wide = d_long.astype(F32)
            masked = jnp.concatenate(
                [
                    jnp.where(wide_group == g, d_wide, 0.0).astype(BF16)
                    for g in range(groups)
                ],
                axis=0,
            )
            pairs = lax.dot_general(
                masked,
                turned.astype(BF16),
                (((1,), (1,)), ((), ())),
                preferred_element_type=F32,
            )
            lines = []
            for g in range(groups):
                one = jnp.where(keep_pair, pairs[g * length : (g + 1) * length], 0.0)
                one = pltpu.roll(one, LANES + 1 - length, 1, stride=1, stride_axis=0)
                lines.append(jnp.sum(one, axis=0, keepdims=True))
            tiles_own[s, 2 * block + 1] = jnp.concatenate(lines, axis=0)
            grads = [jnp.zeros((1, LANES), F32)] * (tap_count + 1)
            for m in range(micro):
                rows = slice(m * length, (m + 1) * length)
                joined_c, scaled, normed, above = saved[m]
                d_short = d_short_all[:, m * LANES : (m + 1) * LANES]
                d_normed = d_short * short[0:1]
                grads[1] = grads[1] + jnp.sum(d_short * normed, axis=0, keepdims=True)
                for j in range(1, tap_count):
                    moved = jnp.where(
                        row_id < total - j, pltpu.roll(d_short, total - j, 0), 0.0
                    )
                    d_normed = d_normed + moved * short[j : j + 1]
                    grads[1 + j] = grads[1 + j] + jnp.sum(
                        moved * normed, axis=0, keepdims=True
                    )
                direct = above * long_out[s, rows, lanes]
                d_normed = jnp.concatenate(
                    [d_normed[:prompt_len], d_normed[prompt_len:] + direct], axis=0
                )
                grads[0] = grads[0] + jnp.sum(d_normed * scaled, axis=0, keepdims=True)
                inner = d_normed[prompt_len:] * gain
                partial[rows, lanes] = inner
                stat_acc[rows, :] += inner * joined_c
            tiles_own[s, 2 * block] = jnp.concatenate(grads, axis=0)
            return carry

        lax.fori_loop(0, blocks, run, 0)

        if direct:
            part_steps(s, lambda copy: copy.start())
            parts_in = tiles_in.at[s]
            parts_in[me_resp] = tiles_own[s, part_slice(me_resp)]

        @pl.when(s > 0)
        def _():
            line = rows_to_line(stat_acc[...])
            all_sums = start_stats(sections + 1 + step, line, line)()[0]
            factor = fac_c[s]
            pull = line_to_rows(all_sums) * (1.0 / width) * factor * factor * factor

            def finish(block, carry):
                lanes = lane_slice(block)
                grad = (
                    upstream[:, lanes]
                    + factor * partial[:, lanes]
                    - rows_in[s, :, lanes].astype(F32) * pull
                )
                upstream[:, lanes] = grad.astype(BF16).astype(F32)
                return carry

            lax.fori_loop(0, blocks, finish, 0)

        if direct:
            part_steps(s, lambda copy: copy.wait())
            tiles_sum[s] = jnp.sum(tiles_in[s], axis=0)

            @pl.when(s == me)
            def _():
                tiles_all[me, me_resp] = tiles_sum[s]

            tile_steps(s, lambda copy: copy.start())

        return carry

    lax.fori_loop(0, sections, backward, 0)

    if direct:
        loop(0, sections, lambda s: tile_steps(s, lambda copy: copy.wait_send()))

        def arrive(step):
            k, r = step // n_resp, step % n_resp

            @pl.when(jnp.logical_not((k == me) & (r == me_resp)))
            def _():
                tile_copy(0, 0, k, r).wait_recv()

        loop(0, sections * n_resp, arrive)
        gain_out, taps_short_out, taps_long_out = outs
        per_line = LANES // groups
        for line in range(sections * blocks // per_line):
            lines = []
            for place in range(per_line):
                block = line * per_line + place
                lanes = slice(block * LANES, (block + 1) * LANES)
                owner, local = divmod(2 * block, 2 * blocks)
                first, second = (divmod(local + kind, share) for kind in range(2))
                tile = tiles_all[owner, first[0], first[1]]
                gain_out[:, lanes] = tile[0:1]
                for j in range(tap_count):
                    taps_short_out[j, :, lanes] = tile[1 + j : 2 + j]
                lines.append(tiles_all[owner, second[0], second[1]])
            lanes = slice(line * LANES, (line + 1) * LANES)
            taps_long_out[0, :, lanes] = jnp.transpose(jnp.concatenate(lines, axis=0))
    else:
        outs[0][...] = tiles_own[...]


def run_kernel(dims, direct, *arrays):
    sections, n_resp, micro, length, prompt_len, chans, per_group, width = dims
    rows = micro * length
    total = prompt_len + length
    group_total = chans // per_group
    tile = (8, LANES)
    tiles = 2 * chans // LANES
    share = tiles // n_resp if direct else 1
    ranks = n_resp if direct else 1
    vmem = pl.BlockSpec(memory_space=pltpu.VMEM)
    hbm = pl.BlockSpec(memory_space=pl.ANY)
    smem = pl.BlockSpec(memory_space=pltpu.SMEM)
    tap_count = arrays[3].shape[0]
    if direct:
        out_shapes = [(1, width), (tap_count, 1, width), (1, LANES, width // per_group)]
    else:
        out_shapes = [(sections, tiles) + tile]
    return pl.pallas_call(
        functools.partial(kernel, dims, direct),
        out_shape=(
            jax.ShapeDtypeStruct(tile, F32),
            *(jax.ShapeDtypeStruct(shape, F32) for shape in out_shapes),
        ),
        in_specs=[hbm, hbm if direct else vmem, hbm, hbm, hbm, smem, vmem, vmem, smem],
        out_specs=(vmem,) * (1 + len(out_shapes)),
        scratch_shapes=[
            pltpu.VMEM((sections, group_total * length, 3 * LANES), BF16),
            pltpu.VMEM((sections, group_total * total, LANES), BF16),
            pltpu.VMEM((sections, ranks, prompt_len, chans), BF16),
            pltpu.VMEM((sections, micro * prompt_len, chans), BF16),
            pltpu.VMEM((sections, 1, chans), F32),
            pltpu.VMEM((sections, tap_count, 1, chans), F32),
            pltpu.VMEM((sections, group_total, 2 * LANES), F32),
            pltpu.VMEM((sections + 1, rows, chans), BF16),
            pltpu.VMEM((sections, total, micro * chans), BF16),
            pltpu.VMEM((sections, rows, chans), F32),
            pltpu.VMEM((sections, micro * prompt_len, LANES), F32),
            pltpu.VMEM((sections, rows, LANES), F32),
            pltpu.VMEM((rows, chans), F32),
            pltpu.VMEM((rows, chans), F32),
            pltpu.VMEM((rows, LANES), F32),
            pltpu.VMEM((rows, LANES), F32),
            pltpu.VMEM((micro * prompt_len, LANES), F32),
            pltpu.VMEM((2 * sections, 2) + tile, F32),
            pltpu.VMEM((2 * sections, sections, 2) + tile, F32),
            pltpu.VMEM(tile, F32),
            pltpu.VMEM((n_resp,) + tile, F32),
            pltpu.VMEM((sections, tiles) + tile, F32),
            pltpu.VMEM((sections, ranks, share) + tile, F32),
            pltpu.VMEM((sections, share) + tile, F32),
            pltpu.VMEM((sections, ranks, share) + tile, F32),
            pltpu.SemaphoreType.DMA((5,)),
            pltpu.SemaphoreType.DMA((2, 3, sections)),
            pltpu.SemaphoreType.DMA((2, sections)),
            pltpu.SemaphoreType.DMA((2, sections, ranks)),
            pltpu.SemaphoreType.DMA((2 * sections, 2, sections)),
            pltpu.SemaphoreType.DMA((2, n_resp)),
            pltpu.SemaphoreType.DMA((2, sections, ranks)),
            pltpu.SemaphoreType.DMA((sections, ranks)),
            pltpu.SemaphoreType.DMA((sections, ranks)),
        ],
        compiler_params=pltpu.CompilerParams(
            has_side_effects=True, vmem_limit_bytes=56 * 1024 * 1024
        ),
    )(*arrays)


def body(
    completion_rows,
    prompt_pool,
    norm_gain,
    short_taps,
    long_taps,
    score_head,
    live_lengths,
    prompt_owner,
    pair_index,
):
    sections = lax.axis_size("section")
    n_resp = lax.axis_size("resp")
    me_resp = lax.axis_index("resp")
    micro, _, length, width = completion_rows.shape
    prompt_len = prompt_pool.shape[2]
    chans = width // sections
    tap_len, group_all = long_taps.shape[1:]
    per_group = width // group_all
    dims = (sections, n_resp, micro, length, prompt_len, chans, per_group, width)

    tiles = 2 * chans // LANES
    direct = n_resp <= 8 and tiles % n_resp == 0

    taps = long_taps[0].T
    flipped = jnp.concatenate([taps[:, :1], taps[:, :0:-1]], axis=1)
    taps = jnp.concatenate([flipped, taps], axis=1)
    prompts = prompt_pool[0, 0]
    if not direct:
        split = prompts.reshape(prompt_len, sections, chans).transpose(1, 0, 2)
        split = lax.all_to_all(split, "section", 0, 0, tiled=True)
        here = (prompt_owner == me_resp)[None, :, None, None]
        split = lax.psum(jnp.where(here, split[:, None], jnp.zeros((), BF16)), "resp")
        prompts = split.reshape(sections, micro * prompt_len, chans)
    rows = completion_rows.reshape(micro * length, width)
    head = score_head[None]

    ends = jnp.pad(
        pair_index.transpose(2, 0, 1),
        ((0, 0), (0, 8 - micro), (0, LANES - pair_index.shape[1])),
        constant_values=-1,
    )
    scores, *grads = run_kernel(
        dims,
        direct,
        rows,
        prompts,
        norm_gain,
        short_taps.transpose(1, 0, 2),
        taps,
        prompt_owner,
        head,
        ends,
        live_lengths,
    )
    scores = scores[:micro, :1].astype(BF16)
    if direct:
        return (scores, grads[0], grads[1].transpose(1, 0, 2), grads[2])
    grads = lax.psum(grads[0], "resp")
    grads = lax.all_to_all(grads, "section", 0, 0, tiled=True)
    grads = grads.reshape(sections * tiles // 2, 2, 8, LANES)
    gs_grad = grads[:, 0].transpose(1, 0, 2).reshape(8, width)
    taps_grad = grads[:, 1].reshape(group_all, tap_len).T
    return (
        scores,
        gs_grad[:1],
        gs_grad[None, 1:],
        taps_grad[None],
    )


def solution(mesh):
    placed = (
        P(None, ("groups", "resp"), None, None),
        P("section", ("groups", "resp"), None, None),
        P("section", None),
        P("section", None, None),
        P("section", None, None),
        P(),
        P(None, ("groups", "resp")),
        P("groups"),
        P(None, "groups", None),
    )
    return jax.shard_map(
        body,
        mesh=mesh,
        in_specs=placed,
        out_specs=(
            P(None, ("groups", "resp")),
            P("section", "groups"),
            P("section", "groups", None),
            P("section", "groups", None),
        ),
        check_vma=False,
    )
```
